128 devices in a mesh: shard: 32 (over z, x, y_hi), tensor: 4 (over y_lo, core).
Axes of the slice: x: 4, y: 4 (y_hi: 2, y_lo: 2; y = y_hi * 2 + y_lo), z: 4, core: 2. Of those that a mesh axis runs over, the one named last changes fastest.
Arguments:
- hidden_acts: bfloat16 [2, 8192, 10944], P(None, 'shard', 'tensor'), may hold values from -18 to 18
- out_grads: bfloat16 [2, 8192, 1024], P(None, 'shard'), may hold values from -18 to 18
- sample_idx: int32 [2, 4096], P(None, 'shard'), may hold values from 0 to 255
- grad_weight: bfloat16 [1024, 10944], P('shard', 'tensor'), may hold values from -112 to 112
- momentum: float32 [1024, 10944], P('shard', 'tensor'), may hold values from -6 to 6
- weight: float32 [1024, 10944], P('shard', 'tensor'), may hold values from -6 to 6
Outputs:
- new_momentum: float32 [1024, 10944], P('shard', 'tensor')
- new_weight: float32 [1024, 10944], P('shard', 'tensor')
The draws below stay inside these ranges and needn't reach their ends.
All inputs are finite; a program needn't handle non-finite values.
Results may differ from the reference program's by a relative error of at most 0.0085.
Values may be sent and summed in bfloat16 or wider, within the bound.
A program may use at most 128 MiB of HBM per device.

```python
import math
import jax
import jax.numpy as jnp
from jax import lax

DOUT = 1024
FF = 10944
ABLK = 1368
NS_STEPS = 2
MBATCH = 2
TOK_DEV = 256
SAMP = 128
TOKENS = 8192
SAMPLES = 4096
N_SHARD = 32


def log_spread(key, count, low, high):
    return jnp.exp(jax.random.uniform(key, (count,), jnp.float32, math.log(low), math.log(high)))


def feature_draw(key, width, latent):
    keys = jax.random.split(key, 7)
    ngroups = TOKENS // TOK_DEV
    token_scale = log_spread(keys[1], MBATCH * TOKENS, 0.5, 2.0).reshape(MBATCH, TOKENS, 1)
    group_cols = log_spread(keys[2], ngroups * width, 0.3, 3.0).reshape(ngroups, width)
    sources = jax.random.randint(keys[4], (4, width), 0, latent)
    signs = (2 * jax.random.randint(keys[5], (4, width), 0, 2) - 1).astype(jnp.float32)
    weights = jax.random.uniform(keys[6], (4, width), jnp.float32, 0.5, 1.0) * signs
    rise = 10.0
    latents = jax.random.truncated_normal(keys[0], -4.0, 4.0, (MBATCH, TOKENS, latent), jnp.float32)
    own = jax.random.truncated_normal(keys[3], -4.0, 4.0, (MBATCH, TOKENS, width), jnp.float32)
    base = 0.5 * own
    for term in range(4):
        base = base + weights[term] * jnp.take(latents, sources[term], axis=2)
    base = 0.5 * base
    base = jnp.clip(base, -3.0, 3.0)
    base = base * token_scale
    group_pos = jnp.arange(ngroups, dtype=jnp.float32) / max(ngroups - 1, 1)
    group_scale = jnp.sqrt((1.0 + (rise - 1.0) * group_pos) / rise)
    factor = group_cols * group_scale[:, None]
    shaped = base.reshape(MBATCH, ngroups, TOK_DEV, width) * factor[None, :, None, :]
    return shaped.reshape(MBATCH, TOKENS, width).astype(jnp.bfloat16)


def draw_hidden_acts(key, part):
    return feature_draw(jax.random.fold_in(key, 3), FF, FF // 4)


def draw_out_grads(key, part):
    return feature_draw(jax.random.fold_in(key, 7), DOUT, DOUT // 2)


def draw_grad_weight(key, part):
    keys = jax.random.split(jax.random.fold_in(key, 11), 3)
    row_pos = jnp.arange(DOUT, dtype=jnp.float32) / DOUT
    col_pos = jnp.arange(FF, dtype=jnp.float32) / FF
    rise = 2.0
    base = jax.random.truncated_normal(keys[0], -4.0, 4.0, (DOUT, FF), jnp.float32)
    row_scale = log_spread(keys[1], DOUT, 0.1, 1.0) * jnp.sqrt(1.0 + rise * row_pos)
    col_scale = log_spread(keys[2], FF, 0.3, 3.0) * jnp.sqrt(1.0 + rise * col_pos)
    return (base * row_scale[:, None] * col_scale[None, :]).astype(jnp.bfloat16)


def touch_ends(array, key, low, high):
    index_at = [jax.random.randint(jax.random.fold_in(key, axis), (), 0, length) for axis, length in enumerate(array.shape)]
    widest = array.shape.index(max(array.shape))
    neighbour = index_at[:widest] + [(index_at[widest] + 1) % array.shape[widest]] + index_at[widest + 1:]
    return array.at[tuple(index_at)].set(low).at[tuple(neighbour)].set(high)


def level_of(own_key, shape, cuts, least, high):
    factor_of = 1.0
    for axis_at, shards_of in cuts:
        draws = jax.random.uniform(jax.random.fold_in(jax.random.fold_in(own_key, 6), axis_at), (shards_of,), jnp.float32, least / len(cuts), high / len(cuts))
        factor_of = factor_of * jnp.repeat(jnp.exp(draws), shape[axis_at] // shards_of).reshape((-1,) + (1,) * (len(shape) - 1 - axis_at))
    return factor_of


def centred(rng, dims, spread, limit, shards=(), kind=jnp.bfloat16):
    values = jax.random.normal(rng, dims, jnp.float32) * spread
    if len(shards) > 0:
        values = level_of(rng, dims, shards, -0.22, 0.18) * values
    return jnp.clip(values, min=-limit, max=limit).astype(kind)


def setup_inputs(seed: int = 0) -> dict:
    key_of = jax.random.split(jax.random.key(seed), 7)
    return {
        "hidden_acts": draw_hidden_acts(jax.random.fold_in(key_of[6], 71), 0),
        "out_grads": draw_out_grads(jax.random.fold_in(key_of[6], 71), 0),
        "sample_idx": touch_ends(jax.random.randint(key_of[2], (MBATCH, SAMPLES), 0, TOK_DEV), jax.random.fold_in(key_of[2], 1), 0, TOK_DEV - 1).astype(jnp.int32),
        "grad_weight": draw_grad_weight(jax.random.fold_in(key_of[6], 71), 0),
        "momentum": centred(key_of[4], (DOUT, FF), 1.0, 6.0, ((0, 32), (1, 4)), jnp.float32),
        "weight": centred(key_of[5], (DOUT, FF), 0.5, 6.0, ((0, 32), (1, 4)), jnp.float32),
    }


DAMPING = 0.1
CLIP_LEVEL = 0.5
MOMENTUM_RATE = 0.9
LEARN_RATE = 0.5

def round_bf16(value):
    return lax.optimization_barrier(value.astype(jnp.bfloat16)).astype(jnp.float32)

def block_moments(rows, width, scale):
    stacked = rows.astype(jnp.float32).reshape(rows.shape[0], rows.shape[1] // width, width)
    moments = jnp.einsum('nkb,nkc->kbc', stacked, stacked)
    return round_bf16(moments * scale)

def newton_inverse(stat):
    width = stat.shape[0]
    shift = DAMPING * jnp.trace(stat) / width
    damped = stat + shift * jnp.eye(width, dtype=jnp.float32)
    normed = (damped / jnp.sqrt(jnp.sum(damped * damped))).astype(jnp.bfloat16)
    iterate = jnp.eye(width, dtype=jnp.bfloat16)
    for step in range(NS_STEPS):
        product = jnp.dot(normed, iterate, preferred_element_type=jnp.float32).astype(jnp.bfloat16)
        twice = 2.0 * iterate.astype(jnp.float32)
        iterate = (twice - jnp.dot(iterate, product, preferred_element_type=jnp.float32)).astype(jnp.bfloat16)
    return iterate

def reference(hidden_acts, out_grads, sample_idx, grad_weight, momentum, weight):
    scale = 1.0 / (MBATCH * SAMPLES)
    index = sample_idx.reshape(MBATCH, N_SHARD, SAMP)
    acts = hidden_acts.reshape(MBATCH, N_SHARD, TOK_DEV, FF)
    grads = out_grads.reshape(MBATCH, N_SHARD, TOK_DEV, DOUT)
    select = jax.vmap(jax.vmap(lambda tokens, where: jnp.take(tokens, where, axis=0)))
    picked_acts = jnp.transpose(select(acts, index), (1, 0, 2, 3))
    picked_grads = jnp.transpose(select(grads, index), (1, 0, 2, 3))

    def add_group(carry, group):
        act_sum, grad_sum = carry
        group_acts, group_grads = group
        act_rows = group_acts.reshape(MBATCH * SAMP, FF)
        grad_rows = group_grads.reshape(MBATCH * SAMP, DOUT)
        act_sum = act_sum + block_moments(act_rows, ABLK, scale)
        grad_sum = grad_sum + block_moments(grad_rows, DOUT, scale)
        return ((act_sum, grad_sum), None)
    start = (jnp.zeros((FF // ABLK, ABLK, ABLK), jnp.float32), jnp.zeros((1, DOUT, DOUT), jnp.float32))
    (act_stat, grad_stat), unused = lax.scan(add_group, start, (picked_acts, picked_grads))
    act_stat = round_bf16(act_stat)
    grad_stat = round_bf16(grad_stat)
    act_inverse = lax.map(newton_inverse, act_stat)
    grad_inverse = newton_inverse(grad_stat[0])
    left = jnp.dot(grad_inverse, grad_weight, preferred_element_type=jnp.float32).astype(jnp.bfloat16)
    left_blocks = left.astype(jnp.float32).reshape(DOUT, FF // ABLK, ABLK)
    update = jnp.einsum('rkb,kbc->rkc', left_blocks, act_inverse.astype(jnp.float32)).reshape(DOUT, FF)
    alignment = jnp.sum(update * grad_weight.astype(jnp.float32))
    ratio = jnp.minimum(1.0, CLIP_LEVEL / jnp.sqrt(alignment / (DOUT * FF)))
    new_momentum = MOMENTUM_RATE * momentum + ratio * update
    new_weight = weight - LEARN_RATE * new_momentum
    return (new_momentum, new_weight)
```

```python
import jax
import jax.numpy as jnp
from jax import lax
from jax.experimental import pallas as pl
from jax.experimental.pallas import tpu as pltpu
from jax.sharding import PartitionSpec as P

DOUT = 1024
FF = 10944
ABLK = 1368
DAMPING = 0.1
CLIP_LEVEL = 0.5
MOMENTUM_RATE = 0.9
LEARN_RATE = 0.5

F32 = jnp.float32
BF16 = jnp.bfloat16
MESH = pl.DeviceIdType.MESH

NT = 11
WIDTH = NT * 128
SPLIT = 1280
EDGE = ABLK - SPLIT
TAIL = 2 * ABLK - 2688
BAND = 6 * 128
ROWS = 96
HALF = ROWS // 2
GT = DOUT // 128
GBAND = 5 * 128
GROWS = 16
MINE = 32


def dot(a, b):
    return lax.dot_general(a, b, (((1,), (0,)), ((), ())), preferred_element_type=F32)


def dot_tn(a, b):
    return lax.dot_general(a, b, (((0,), (0,)), ((), ())), preferred_element_type=F32)


def fold_rows(value):
    return value.reshape(value.shape[0] // 8, 8, value.shape[1]).sum(0)


def total(value):
    return jnp.sum(jnp.sum(value, axis=1, keepdims=True), axis=0, keepdims=True)


def kernel(
    idx_ref, grads_ref, w_ref, acts_ref,
    upd_out, align_out,
    picked, gpicked, part, w2, wpair, wc, edge,
    gq, grecv, gall, gfull,
    rb1, st1, r1, rb2, st2, r2, r3,
    ag, sfull, vt, vfull, left, upd, ux, al, al1, al2,
    grs_s, grs_r, gag_s, gag_r, gx_s, gx_r, wa_s, wa_r, lf_s, lf_r,
    ring_s, ring_r, a1_s, a1_r, a2_s, a2_r, one_s, one_r,
):
    s = lax.axis_index("shard")
    t = lax.axis_index("tensor")
    z, x, h, o = s // 8, (s // 2) % 4, s % 2, s // 2
    pair = o * 2 + (1 - h)
    scale = 1.0 / 8192.0
    lane = lax.broadcasted_iota(jnp.int32, (1, 128), 1)

    def copy_to(src, dst, send, recv, shard, tensor=None):
        return pltpu.make_async_remote_copy(
            src_ref=src, dst_ref=dst, send_sem=send, recv_sem=recv,
            device_id=(shard, t if tensor is None else tensor), device_id_type=MESH,
        )

    def wait_bytes(ref, sem):
        pltpu.make_async_copy(ref, ref, sem).wait()

    barrier = pltpu.get_barrier_semaphore()

    @pl.loop(0, 32)
    def _(i):
        @pl.when(i != s)
        def _():
            pl.semaphore_signal(barrier, inc=1, device_id=(i, t), device_id_type=MESH)

    for d in range(1, 4):
        pl.semaphore_signal(barrier, inc=1, device_id=(s, (t + d) % 4), device_id_type=MESH)

    hots = []
    for m in range(2):
        token = lax.broadcasted_iota(jnp.int32, (256, 128), 0)
        hots.append(jnp.where(token == idx_ref[m:m + 1, :], 1.0, 0.0).astype(BF16))
    for m in range(2):
        rows = slice(128 * m, 128 * m + 128)
        pg = dot_tn(hots[m], grads_ref[m]).astype(BF16)
        gpicked[rows, 0:DOUT] = pg
        gpicked[rows, DOUT:DOUT + 512] = pg[:, 0:512]
    for i in range(2):
        at = pl.multiple_of(128 * (2 * t + i), 128)
        strip = dot_tn(gpicked[:, pl.ds(at, 128)], gpicked[:, pl.ds(at, GBAND)])
        gq[128 * i:128 * i + 128, :] = (strip * scale).astype(BF16)

    for j in range(NT - 1):
        w2[0, j] = w_ref[:, 128 * j:128 * j + 128]
        w2[1, j] = w_ref[:, WIDTH + 128 * j:WIDTH + 128 * j + 128]
    cut = w_ref[:, SPLIT:WIDTH].astype(F32)
    w2[0, NT - 1] = jnp.where(lane < EDGE, cut, 0.0).astype(BF16)
    edge[0:32, :] = jnp.where(lane >= EDGE, cut, 0.0)
    edge[0:32, 0:TAIL] = w_ref[:, 2688:2736].astype(F32)
    w2[1, NT - 1] = edge[0:32, :].astype(BF16)
    wpair[:, pl.ds(pl.multiple_of(32 * h, 32), 32), :] = w2[h]

    pl.semaphore_wait(barrier, 34)

    g_lane = t % 2
    is_gowner = h == g_lane

    @pl.loop(0, 16)
    def _(i):
        to = 2 * i + g_lane

        @pl.when(to != s)
        def _():
            copy_to(gq.at[pl.ds(pl.multiple_of(GROWS * i, GROWS), GROWS)], grecv.at[s],
                    grs_s.at[i], grs_r.at[0], to).start()

    for b in range(2):
        @pl.loop(0, NT)
        def _(j):
            to = 2 * j + b

            @pl.when(to != s)
            def _():
                copy_to(w2.at[b, j], wc.at[pl.ds(pl.multiple_of(32 * s, 32), 32)],
                        wa_s.at[b * NT + j], wa_r.at[0], to).start()

    active = o < NT

    @pl.when(active)
    def _():
        wc[pl.ds(pl.multiple_of(32 * s, 32), 32), :] = w2[h, jnp.minimum(o, NT - 1)]

    wp_copy = copy_to(w2.at[1 - h], wpair.at[:, pl.ds(pl.multiple_of(32 * h, 32), 32), :],
                      one_s.at[0], one_r.at[0], pair)
    wp_copy.start()

    @pl.when(is_gowner)
    def _():
        grecv[s] = gq[pl.ds(pl.multiple_of(GROWS * o, GROWS), GROWS), :]

    def ring_ids(axis):
        if axis == 0:
            return x, z * 8 + ((x + 1) % 4) * 2 + h, z * 8 + ((x + 3) % 4) * 2 + h
        return z, ((z + 1) % 4) * 8 + x * 2 + h, ((z + 3) % 4) * 8 + x * 2 + h

    part[0, 2, 3, 64:96] = jnp.zeros((32, BAND), BF16)
    part[0, 3, 3] = jnp.zeros((96, BAND), BF16)
    part[1, 3, 2, 64:96] = jnp.zeros((32, BAND), BF16)
    part[1, 3, 3] = jnp.zeros((96, BAND), BF16)

    pending = []

    def ring(k, src, dst, to):
        c = copy_to(src, dst, ring_s.at[k], ring_r.at[k], to)
        c.start()
        pending.append(c)
        return c

    phase1 = []
    for c in range(2):
        for m in range(2):
            rows = slice(128 * m, 128 * m + 128)
            if c == 0:
                pa = dot_tn(hots[m], acts_ref[m, :, 0:WIDTH])
                picked[c, rows, 0:SPLIT] = pa[:, 0:SPLIT].astype(BF16)
                edge[rows, :] = jnp.where(lane < EDGE, pa[:, SPLIT:WIDTH], 0.0)
                cut = jnp.where(lane >= EDGE, pa[:, SPLIT:WIDTH], 0.0)
                picked[c, rows, SPLIT:WIDTH] = edge[rows, :].astype(BF16)
                edge[rows, :] = cut
            else:
                pa = dot_tn(hots[m], acts_ref[m, :, WIDTH:2 * ABLK])
                picked[c, rows, 0:SPLIT] = pa[:, 0:SPLIT].astype(BF16)
                edge[rows, 0:TAIL] = pa[:, SPLIT:SPLIT + TAIL]
                picked[c, rows, SPLIT:WIDTH] = edge[rows, :].astype(BF16)
        picked[c, :, WIDTH:WIDTH + 640] = picked[c, :, 0:640]

        @pl.loop(0, NT)
        def _(i):
            at = pl.multiple_of(128 * i, 128)
            strip = dot_tn(picked[c, :, pl.ds(at, 128)], picked[c, :, pl.ds(at, BAND)])
            strip = (strip * scale).astype(BF16)
            for q in range(4):
                u = 4 * i + q
                oo = u // 3
                row = pl.multiple_of((u % 3) * 32, 32)
                zz, xx = oo // 4, oo % 4
                piece = strip[32 * q:32 * q + 32]
                if c == 0:
                    part[0, xx, zz, pl.ds(row, 32), :] = piece
                else:
                    part[1, zz, xx, pl.ds(row, 32), :] = piece

        pos, right, left_id = ring_ids(c)
        far, nxt, prv = (pos + 2) % 4, (pos + 1) % 4, (pos + 3) % 4
        k = 6 * c
        top, bottom = pl.ds(0, HALF), pl.ds(HALF, HALF)
        phase1.append([
            ring(k + 0, part.at[c, far, :, top], rb1.at[c, 0], right),
            ring(k + 1, part.at[c, far, :, bottom], rb1.at[c, 1], left_id),
            ring(k + 2, part.at[c, nxt, :, bottom], rb1.at[c, 2], right),
            ring(k + 3, part.at[c, prv, :, top], rb1.at[c, 3], left_id),
        ])

    @pl.when(is_gowner)
    def _():
        wait_bytes(grecv.at[pl.ds(0, 31)], grs_r.at[0])
        acc = grecv[0].astype(F32)
        for i in range(1, 32):
            acc = acc + grecv[i].astype(F32)
        gall[pl.ds(pl.multiple_of(256 * t + GROWS * o, GROWS), GROWS), :] = acc.astype(BF16)

        @pl.loop(0, 32)
        def _(i):
            @pl.when(i != s)
            def _():
                mine = gall.at[pl.ds(pl.multiple_of(256 * t + GROWS * o, GROWS), GROWS)]
                copy_to(mine, mine, gag_s.at[i], gag_r.at[0], i).start()

    def add2(a, b):
        return a.astype(F32) + b.astype(F32)

    def add3(a, b, c):
        return a.astype(F32) + b.astype(F32) + c.astype(F32)

    for c in range(2):
        pos, right, left_id = ring_ids(c)
        nxt, prv = (pos + 1) % 4, (pos + 3) % 4
        k = 6 * c
        phase1[c][0].wait_recv()
        for y in range(4):
            st1[c, 0, y] = add2(rb1[c, 0, y], part[c, nxt, y, 0:HALF]).astype(BF16)
        phase1[c].append(ring(k + 4, st1.at[c, 0], rb1.at[c, 4], right))
        phase1[c][1].wait_recv()
        for y in range(4):
            st1[c, 1, y] = add2(rb1[c, 1, y], part[c, prv, y, HALF:ROWS]).astype(BF16)
        phase1[c].append(ring(k + 5, st1.at[c, 1], rb1.at[c, 5], left_id))

    @pl.when(is_gowner)
    def _():
        wait_bytes(gall.at[pl.ds(0, 240)], gag_r.at[0])

    @pl.when(jnp.logical_not(is_gowner))
    def _():
        wait_bytes(gall.at[pl.ds(0, 256)], gag_r.at[0])

    gx = []
    for d in range(1, 4):
        mine = gall.at[pl.ds(pl.multiple_of(256 * t, 256), 256)]
        g = copy_to(mine, mine, gx_s.at[d], gx_r.at[d], s, (t + d) % 4)
        g.start()
        gx.append(g)

    phase2 = []
    for c in range(2):
        pos, right, left_id = ring_ids(c)
        for cp in phase1[c][2:]:
            cp.wait_recv()
        for y in range(4):
            r1[c, y, 0:HALF] = add3(part[c, pos, y, 0:HALF], rb1[c, 4, y], rb1[c, 3, y]).astype(BF16)
            r1[c, y, HALF:ROWS] = add3(part[c, pos, y, HALF:ROWS], rb1[c, 5, y], rb1[c, 2, y]).astype(BF16)
        pos, right, left_id = ring_ids(1 - c)
        far, nxt, prv = (pos + 2) % 4, (pos + 1) % 4, (pos + 3) % 4
        k = 12 + 6 * c
        phase2.append([
            ring(k + 0, r1.at[c, far, top], rb2.at[c, 0], right),
            ring(k + 1, r1.at[c, far, bottom], rb2.at[c, 1], left_id),
            ring(k + 2, r1.at[c, nxt, bottom], rb2.at[c, 2], right),
            ring(k + 3, r1.at[c, prv, top], rb2.at[c, 3], left_id),
        ])
    for c in range(2):
        pos, right, left_id = ring_ids(1 - c)
        nxt, prv = (pos + 1) % 4, (pos + 3) % 4
        k = 12 + 6 * c
        phase2[c][0].wait_recv()
        st2[c, 0] = add2(rb2[c, 0], r1[c, nxt, 0:HALF]).astype(BF16)
        phase2[c].append(ring(k + 4, st2.at[c, 0], rb2.at[c, 4], right))
        phase2[c][1].wait_recv()
        st2[c, 1] = add2(rb2[c, 1], r1[c, prv, HALF:ROWS]).astype(BF16)
        phase2[c].append(ring(k + 5, st2.at[c, 1], rb2.at[c, 5], left_id))
    for c in range(2):
        pos, right, left_id = ring_ids(1 - c)
        for cp in phase2[c][2:]:
            cp.wait_recv()
        r2[c, 0:HALF] = add3(r1[c, pos, 0:HALF], rb2[c, 4], rb2[c, 3]).astype(BF16)
        r2[c, HALF:ROWS] = add3(r1[c, pos, HALF:ROWS], rb2[c, 5], rb2[c, 2]).astype(BF16)

    hx = ring(24, r2.at[1 - h], r3, pair)
    hx.wait_recv()
    ag[pl.ds(pl.multiple_of(ROWS * o, ROWS), ROWS), :] = add2(r2[h], r3[...]).astype(BF16)

    def piece(axis, first, second, k):
        zz, xx = (second, first) if axis == 0 else (first, second)
        return ag.at[pl.ds(pl.multiple_of(ROWS * (4 * zz + xx) + HALF * k, HALF), HALF)]

    def cols(ref, side):
        return ref.at[:, pl.ds(384 * side, 384)]

    lines = []
    for k in range(2):
        pa, ra, la = ring_ids(k)
        pb, rb, lb = ring_ids(1 - k)
        base = 25 + 16 * k
        own = piece(k, pa, pb, k)
        lines.append({"a": [ring(base, own, own, ra), ring(base + 1, own, own, la)], "r": [], "l": []})

    def send_b(k, n, first):
        pb, rb, lb = ring_ids(1 - k)
        base = 25 + 16 * k
        p = piece(k, first, pb, k)
        lines[k]["r"].append(ring(base + 4 + n, p, p, rb))
        lines[k]["l"].append(ring(base + 8 + n, p, p, lb))

    for k in range(2):
        send_b(k, 0, ring_ids(k)[0])
    for k in range(2):
        pa, ra, la = ring_ids(k)
        pb = ring_ids(1 - k)[0]
        base = 25 + 16 * k
        lines[k]["a"][0].wait_recv()
        p = cols(piece(k, (pa + 3) % 4, pb, k), 0)
        lines[k]["a"].append(ring(base + 2, p, p, ra))
        lines[k]["a"][1].wait_recv()
        p = cols(piece(k, (pa + 1) % 4, pb, k), 1)
        lines[k]["a"].append(ring(base + 3, p, p, la))
    for k in range(2):
        pa = ring_ids(k)[0]
        send_b(k, 1, (pa + 3) % 4)
        send_b(k, 2, (pa + 1) % 4)
    for k in range(2):
        pa = ring_ids(k)[0]
        lines[k]["a"][2].wait_recv()
        lines[k]["a"][3].wait_recv()
        send_b(k, 3, (pa + 2) % 4)
    order = (0, 3, 1, 2)
    for n in range(2):
        for k in range(2):
            pa = ring_ids(k)[0]
            pb, rb, lb = ring_ids(1 - k)
            base = 25 + 16 * k
            lines[k]["r"][n].wait_recv()
            p = piece(k, (pa + order[n]) % 4, (pb + 3) % 4, k)
            lines[k]["a"].append(ring(base + 12 + n, p, p, rb))

    for g in gx:
        g.wait_recv()
    eye = lax.broadcasted_iota(jnp.int32, (128, 128), 0) == lax.broadcasted_iota(jnp.int32, (128, 128), 1)

    def unpack(src, dst, tiles, band, double):
        bands = band // 128
        column = lax.broadcasted_iota(jnp.int32, (1, band), 1) // 128
        weight = jnp.where(jnp.logical_and(column > 0, column <= double), 2.0, 1.0)

        def body(i, carry):
            square, trace = carry
            at = pl.multiple_of(128 * i, 128)
            strip = src[pl.ds(at, 128), :]
            wide = strip.astype(F32)
            square = square + fold_rows(wide * wide) * weight
            trace = trace + fold_rows(jnp.where(eye, wide[:, 0:128], 0.0))
            for k in range(bands):
                to = pl.multiple_of(128 * ((i + k) % tiles), 128)
                dst[pl.ds(at, 128), pl.ds(to, 128)] = strip[:, 128 * k:128 * k + 128]
                if 1 <= k <= double:
                    dst[pl.ds(to, 128), pl.ds(at, 128)] = wide[:, 128 * k:128 * k + 128].T.astype(BF16)
            return square, trace

        square, trace = lax.fori_loop(
            0, tiles, body, (jnp.zeros((8, band), F32), jnp.zeros((8, 128), F32)))
        return total(square), total(trace)

    def norms(square, trace, width):
        shift = DAMPING * trace / width
        return shift, 1.0 / jnp.sqrt(square + 2.0 * shift * trace + shift * shift * width)

    @pl.when(active)
    def _():
        square, trace = unpack(gall, gfull, GT, GBAND, 3)
        shift, inv = norms(square, trace, float(DOUT))
        wait_bytes(wc.at[pl.ds(0, 31 * 32)], wa_r.at[0])
        y0 = wc[...].astype(F32)
        y1 = (dot(gfull[...], wc[...]) + shift * y0) * inv
        left[...] = y1.astype(BF16)
        y2 = (dot(gfull[...], left[...]) + shift * y1) * inv
        left[...] = y2.astype(BF16)
        y3 = (dot(gfull[...], left[...]) + shift * y2) * inv
        left[...] = (4.0 * y0 - 6.0 * y1 + 4.0 * y2 - y3).astype(BF16)
        vt[o] = left[pl.ds(pl.multiple_of(64 * o, 64), 64), :]

        @pl.loop(0, 16)
        def _(i):
            @pl.when(i != o)
            def _():
                copy_to(left.at[pl.ds(pl.multiple_of(64 * i, 64), 64)], vt.at[o],
                        lf_s.at[i], lf_r.at[0], 2 * i + h).start()

    for n in range(2, 4):
        for k in range(2):
            pa = ring_ids(k)[0]
            pb, rb, lb = ring_ids(1 - k)
            base = 25 + 16 * k
            lines[k]["l"][n].wait_recv()
            p = piece(k, (pa + order[n]) % 4, (pb + 1) % 4, k)
            lines[k]["a"].append(ring(base + 12 + n, p, p, lb))
    for k in range(2):
        for n in range(2, 4):
            lines[k]["r"][n].wait_recv()
        for n in range(2):
            lines[k]["l"][n].wait_recv()
        for cp in lines[k]["a"][4:]:
            cp.wait_recv()

    square, trace = unpack(ag, sfull, NT, BAND, 5)
    shift, inv = norms(square, trace, float(ABLK))

    @pl.when(active)
    def _():
        wait_bytes(vt.at[pl.ds(0, NT - 1)], lf_r.at[0])

    @pl.when(jnp.logical_not(active))
    def _():
        wait_bytes(vt, lf_r.at[0])

    for j in range(NT):
        vfull[:, 128 * j:128 * j + 128] = vt[j]
    y0 = vfull[...].astype(F32)
    y1 = (dot(vfull[...], sfull[...]) + shift * y0) * inv
    vfull[...] = y1.astype(BF16)
    upd[...] = 4.0 * y0 - 6.0 * y1
    y2 = (dot(vfull[...], sfull[...]) + shift * y1) * inv
    vfull[...] = y2.astype(BF16)
    upd[...] = upd[...] + 4.0 * y2
    y3 = (dot(vfull[...], sfull[...]) + shift * y2) * inv
    upd[...] = upd[...] - y3

    u_copy = copy_to(upd.at[pl.ds(pl.multiple_of(32 * (1 - h), 32), 32)], ux, one_s.at[1], one_r.at[1], pair)
    u_copy.start()

    wp_copy.wait_recv()
    acc = jnp.zeros((64, 128), F32)
    for j in range(NT):
        acc = acc + upd[:, 128 * j:128 * j + 128] * wpair[j].astype(F32)
    al[0] = fold_rows(acc)
    al1[t] = al[0]
    sums = []
    for d in range(1, 4):
        g = copy_to(al.at[0], al1.at[t], a1_s.at[d], a1_r.at[d], s, (t + d) % 4)
        g.start()
        sums.append(g)
    for g in sums:
        g.wait_recv()
    al[1] = (al1[0] + al1[1]) + (al1[2] + al1[3])
    al2[s] = al[1]

    @pl.loop(0, 32)
    def _(i):
        @pl.when(i != s)
        def _():
            copy_to(al.at[1], al2.at[s], a2_s.at[i], a2_r.at[0], i).start()

    u_copy.wait_recv()
    own = upd[pl.ds(pl.multiple_of(32 * h, 32), 32), :]
    other = ux[...]
    b0 = jnp.where(h == 0, own, other)
    b1 = jnp.where(h == 0, other, own)
    upd_out[:, 0:SPLIT] = b0[:, 0:SPLIT]
    upd_out[:, SPLIT:WIDTH] = jnp.where(lane < EDGE, b0[:, SPLIT:WIDTH], b1[:, SPLIT:WIDTH])
    upd_out[:, WIDTH:2688] = b1[:, 0:SPLIT]
    upd_out[:, 2688:2736] = b1[:, SPLIT:SPLIT + TAIL]

    wait_bytes(al2.at[pl.ds(0, 31)], a2_r.at[0])
    acc = al2[0]
    for i in range(1, 32):
        acc = acc + al2[i]
    align_out[...] = jnp.broadcast_to(total(acc), (8, 128))

    for cp in pending + gx + sums + [wp_copy, u_copy]:
        cp.wait_send()

    @pl.loop(0, 16)
    def _(i):
        @pl.when(2 * i + g_lane != s)
        def _():
            wait_bytes(gq.at[pl.ds(0, GROWS)], grs_s.at[i])

        @pl.when(jnp.logical_and(active, i != o))
        def _():
            wait_bytes(left.at[pl.ds(0, 64)], lf_s.at[i])

    for b in range(2):
        @pl.loop(0, NT)
        def _(j):
            @pl.when(2 * j + b != s)
            def _():
                wait_bytes(w2.at[b, j], wa_s.at[b * NT + j])

    @pl.loop(0, 32)
    def _(i):
        @pl.when(i != s)
        def _():
            wait_bytes(al.at[1], a2_s.at[i])

        @pl.when(jnp.logical_and(is_gowner, i != s))
        def _():
            wait_bytes(gall.at[pl.ds(0, GROWS)], gag_s.at[i])


def whole_step(sample_idx, out_grads, grad_weight, hidden_acts):
    dma = pltpu.SemaphoreType.DMA
    vmem = pltpu.VMEM
    return pl.pallas_call(
        kernel,
        out_shape=(
            jax.ShapeDtypeStruct((MINE, 2 * ABLK), F32),
            jax.ShapeDtypeStruct((8, 128), F32),
        ),
        in_specs=[pl.BlockSpec(memory_space=pltpu.VMEM)] * 4,
        out_specs=(pl.BlockSpec(memory_space=pltpu.VMEM),) * 2,
        scratch_shapes=[
            vmem((2, 256, WIDTH + 640), BF16),
            vmem((256, DOUT + 512), BF16),
            vmem((2, 4, 4, ROWS, BAND), BF16),
            vmem((2, NT, 32, 128), BF16),
            vmem((NT, 64, 128), BF16),
            vmem((DOUT, 128), BF16),
            vmem((256, 128), F32),
            vmem((256, GBAND), BF16),
            vmem((32, GROWS, GBAND), BF16),
            vmem((DOUT, GBAND), BF16),
            vmem((DOUT, DOUT), BF16),
            vmem((2, 6, 4, HALF, BAND), BF16),
            vmem((2, 2, 4, HALF, BAND), BF16),
            vmem((2, 4, ROWS, BAND), BF16),
            vmem((2, 6, HALF, BAND), BF16),
            vmem((2, 2, HALF, BAND), BF16),
            vmem((2, ROWS, BAND), BF16),
            vmem((ROWS, BAND), BF16),
            vmem((16 * ROWS, BAND), BF16),
            vmem((WIDTH, WIDTH), BF16),
            vmem((NT, 64, 128), BF16),
            vmem((64, WIDTH), BF16),
            vmem((DOUT, 128), BF16),
            vmem((64, WIDTH), F32),
            vmem((32, WIDTH), F32),
            vmem((2, 8, 128), F32),
            vmem((4, 8, 128), F32),
            vmem((32, 8, 128), F32),
            dma((16,)), dma((1,)),
            dma((32,)), dma((1,)),
            dma((4,)), dma((4,)),
            dma((2 * NT,)), dma((1,)),
            dma((16,)), dma((1,)),
            dma((57,)), dma((57,)),
            dma((4,)), dma((4,)),
            dma((32,)), dma((1,)),
            dma((2,)), dma((2,)),
        ],
        compiler_params=pltpu.CompilerParams(
            collective_id=0, has_side_effects=True, vmem_limit_bytes=60 * 1024 * 1024),
    )(sample_idx, out_grads, grad_weight, hidden_acts)


def per_device(hidden_acts, out_grads, sample_idx, grad_weight, momentum, weight):
    update, alignment = whole_step(sample_idx, out_grads, grad_weight, hidden_acts)
    ratio = jnp.minimum(1.0, CLIP_LEVEL / jnp.sqrt(alignment[0, 0] / (DOUT * FF)))
    new_momentum = MOMENTUM_RATE * momentum + ratio * update
    new_weight = weight - LEARN_RATE * new_momentum
    return (new_momentum, new_weight)


def solution(mesh):
    in_specs = (
        P(None, "shard", "tensor"),
        P(None, "shard", None),
        P(None, "shard"),
        P("shard", "tensor"),
        P("shard", "tensor"),
        P("shard", "tensor"),
    )
    out_specs = (P("shard", "tensor"), P("shard", "tensor"))
    return jax.shard_map(
        per_device, mesh=mesh, in_specs=in_specs, out_specs=out_specs, check_vma=False
    )
```

```python
import jax
import jax.numpy as jnp
from jax import lax
from jax.experimental import pallas as pl
from jax.experimental.pallas import tpu as pltpu
from jax.sharding import PartitionSpec as P

DOUT = 1024
FF = 10944
ABLK = 1368
DAMPING = 0.1
CLIP_LEVEL = 0.5
MOMENTUM_RATE = 0.9
LEARN_RATE = 0.5

F32 = jnp.float32
BF16 = jnp.bfloat16
MESH = pl.DeviceIdType.MESH

NT = 11
WIDTH = NT * 128
SPLIT = 1280
EDGE = ABLK - SPLIT
TAIL = 2 * ABLK - 2688
BAND = 6 * 128
ROWS = 96
HALF = ROWS // 2
GT = DOUT // 128
GBAND = 5 * 128
GROWS = 16
MINE = 32


def dot(a, b):
    return lax.dot_general(a, b, (((1,), (0,)), ((), ())), preferred_element_type=F32)


def dot_tn(a, b):
    return lax.dot_general(a, b, (((0,), (0,)), ((), ())), preferred_element_type=F32)


def fold_rows(value):
    return value.reshape(value.shape[0] // 8, 8, value.shape[1]).sum(0)


def dot_nt(a, b):
    return lax.dot_general(a, b, (((1,), (1,)), ((), ())), preferred_element_type=F32)


def total(value):
    return jnp.sum(jnp.sum(value, axis=1, keepdims=True), axis=0, keepdims=True)


def kernel(
    idx_ref, grads_hbm, w_hbm, acts_hbm,
    upd_out,
    grads_ref, w_ref, acts_ref,
    picked, gpicked, part, w2, wpair, wc, edge,
    gq, grecv, gall, gfull,
    rb1, st1, r1, rb2, st2, r2, r3,
    ag, sfull, vt, vfull, left, upd, ux, al, al1, al2,
    grs_s, grs_r, gag_s, gag_r, gx_s, gx_r, wa_s, wa_r, lf_s, lf_r,
    ring_s, ring_r, a1_s, a1_r, a2_s, a2_r, one_s, one_r, in_s,
):
    s = lax.axis_index("shard")
    t = lax.axis_index("tensor")
    z, x, h, o = s // 8, (s // 2) % 4, s % 2, s // 2
    pair = o * 2 + (1 - h)
    scale = 1.0 / 8192.0
    lane = lax.broadcasted_iota(jnp.int32, (1, 128), 1)

    def copy_to(src, dst, send, recv, shard, tensor=None):
        return pltpu.make_async_remote_copy(
            src_ref=src, dst_ref=dst, send_sem=send, recv_sem=recv,
            device_id=(shard, t if tensor is None else tensor), device_id_type=MESH,
        )

    def wait_bytes(ref, sem):
        pltpu.make_async_copy(ref, ref, sem).wait()

    loads = [
        pltpu.make_async_copy(grads_hbm, grads_ref, in_s.at[0]),
        pltpu.make_async_copy(w_hbm, w_ref, in_s.at[1]),
        pltpu.make_async_copy(acts_hbm, acts_ref, in_s.at[2]),
    ]
    for load in loads:
        load.start()

    barrier = pltpu.get_barrier_semaphore()

    @pl.loop(0, 32)
    def _(i):
        @pl.when(i != s)
        def _():
            pl.semaphore_signal(barrier, inc=1, device_id=(i, t), device_id_type=MESH)

    for d in range(1, 4):
        pl.semaphore_signal(barrier, inc=1, device_id=(s, (t + d) % 4), device_id_type=MESH)
    across = 2 * (1 - t // 2) + t % 2
    pl.semaphore_signal(barrier, inc=1, device_id=(pair, across), device_id_type=MESH)

    hots = []
    for m in range(2):
        token = lax.broadcasted_iota(jnp.int32, (256, 128), 0)
        hots.append(jnp.where(token == idx_ref[m:m + 1, :], 1.0, 0.0).astype(BF16))
    loads[0].wait()
    for m in range(2):
        rows = slice(128 * m, 128 * m + 128)
        pg = dot_tn(hots[m], grads_ref[m]).astype(BF16)
        gpicked[rows, 0:DOUT] = pg
        gpicked[rows, DOUT:DOUT + 512] = pg[:, 0:512]
    for i in range(2):
        at = pl.multiple_of(128 * (2 * t + i), 128)
        strip = dot_tn(gpicked[:, pl.ds(at, 128)], gpicked[:, pl.ds(at, GBAND)])
        gq[128 * i:128 * i + 128, :] = (strip * scale).astype(BF16)

    loads[1].wait()
    for j in range(NT - 1):
        w2[0, j] = w_ref[:, 128 * j:128 * j + 128]
        w2[1, j] = w_ref[:, WIDTH + 128 * j:WIDTH + 128 * j + 128]
    cut = w_ref[:, SPLIT:WIDTH].astype(F32)
    w2[0, NT - 1] = jnp.where(lane < EDGE, cut, 0.0).astype(BF16)
    edge[0:32, 0:128] = jnp.where(lane >= EDGE, cut, 0.0)
    edge[0:32, 0:TAIL] = w_ref[:, 2688:2736].astype(F32)
    w2[1, NT - 1] = edge[0:32, 0:128].astype(BF16)
    wpair[:, pl.ds(pl.multiple_of(32 * h, 32), 32), :] = w2[h]

    pl.semaphore_wait(barrier, 35)

    g_lane = t % 2
    is_gowner = h == g_lane

    @pl.loop(0, 16)
    def _(i):
        to = 2 * i + g_lane

        @pl.when(to != s)
        def _():
            copy_to(gq.at[pl.ds(pl.multiple_of(GROWS * i, GROWS), GROWS)], grecv.at[s],
                    grs_s.at[i], grs_r.at[0], to).start()

    for b in range(2):
        @pl.loop(0, NT)
        def _(j):
            to = 2 * j + b

            @pl.when(to != s)
            def _():
                copy_to(w2.at[b, j], wc.at[pl.ds(pl.multiple_of(32 * s, 32), 32)],
                        wa_s.at[b * NT + j], wa_r.at[0], to).start()

    active = o < NT

    @pl.when(active)
    def _():
        wc[pl.ds(pl.multiple_of(32 * s, 32), 32), :] = w2[h, jnp.minimum(o, NT - 1)]

    wp_copy = copy_to(w2.at[1 - h], wpair.at[:, pl.ds(pl.multiple_of(32 * h, 32), 32), :],
                      one_s.at[0], one_r.at[0], pair)
    wp_copy.start()

    @pl.when(is_gowner)
    def _():
        grecv[s] = gq[pl.ds(pl.multiple_of(GROWS * o, GROWS), GROWS), :]

    def ring_ids(axis):
        if axis == 0:
            return x, z * 8 + ((x + 1) % 4) * 2 + h, z * 8 + ((x + 3) % 4) * 2 + h
        return z, ((z + 1) % 4) * 8 + x * 2 + h, ((z + 3) % 4) * 8 + x * 2 + h

    part[0, 2, 3, 64:96] = jnp.zeros((32, BAND), BF16)
    part[0, 3, 3] = jnp.zeros((96, BAND), BF16)
    part[1, 3, 2, 64:96] = jnp.zeros((32, BAND), BF16)
    part[1, 3, 3] = jnp.zeros((96, BAND), BF16)

    pending = []
    loads[2].wait()
    high = lax.broadcasted_iota(jnp.int32, (128, 1), 0) >= EDGE

    def ring(k, src, dst, to):
        c = copy_to(src, dst, ring_s.at[k], ring_r.at[k], to)
        c.start()
        pending.append(c)
        return c

    phase1 = []
    for c in range(2):
        for m in range(2):
            cols_m = slice(128 * m, 128 * m + 128)
            if c == 0:
                pa = dot(acts_ref[m, 0:WIDTH, :], hots[m])
                picked[c, 0:SPLIT, cols_m] = pa[0:SPLIT].astype(BF16)
                cut = pa[SPLIT:WIDTH]
                picked[c, SPLIT:WIDTH, cols_m] = jnp.where(high, 0.0, cut).astype(BF16)
                edge[:, cols_m] = jnp.where(high, cut, 0.0)
            else:
                pa = dot(acts_ref[m, WIDTH:2 * ABLK, :], hots[m])
                picked[c, 0:SPLIT, cols_m] = pa[0:SPLIT].astype(BF16)
                edge[0:TAIL, cols_m] = pa[SPLIT:SPLIT + TAIL]
                picked[c, SPLIT:WIDTH, cols_m] = edge[:, cols_m].astype(BF16)
        picked[c, WIDTH:WIDTH + 640, :] = picked[c, 0:640, :]

        @pl.loop(0, NT)
        def _(i):
            at = pl.multiple_of(128 * i, 128)
            strip = dot_nt(picked[c, pl.ds(at, 128), :], picked[c, pl.ds(at, BAND), :])
            strip = (strip * scale).astype(BF16)
            for q in range(4):
                u = 4 * i + q
                oo = u // 3
                row = pl.multiple_of((u % 3) * 32, 32)
                zz, xx = oo // 4, oo % 4
                piece = strip[32 * q:32 * q + 32]
                if c == 0:
                    part[0, xx, zz, pl.ds(row, 32), :] = piece
                else:
                    part[1, zz, xx, pl.ds(row, 32), :] = piece

        if c == 0:
            @pl.when(is_gowner)
            def _():
                wait_bytes(grecv.at[pl.ds(0, 31)], grs_r.at[0])
                acc = grecv[0].astype(F32)
                for i in range(1, 32):
                    acc = acc + grecv[i].astype(F32)
                gall[pl.ds(pl.multiple_of(256 * t + GROWS * o, GROWS), GROWS), :] = acc.astype(BF16)

                @pl.loop(0, 32)
                def _(i):
                    @pl.when(i != s)
                    def _():
                        mine = gall.at[pl.ds(pl.multiple_of(256 * t + GROWS * o, GROWS), GROWS)]
                        copy_to(mine, mine, gag_s.at[i], gag_r.at[0], i).start()

        pos, right, left_id = ring_ids(c)
        far, nxt, prv = (pos + 2) % 4, (pos + 1) % 4, (pos + 3) % 4
        k = 6 * c
        top, bottom = pl.ds(0, HALF), pl.ds(HALF, HALF)
        phase1.append([
            ring(k + 0, part.at[c, far, :, top], rb1.at[c, 0], right),
            ring(k + 1, part.at[c, far, :, bottom], rb1.at[c, 1], left_id),
            ring(k + 2, part.at[c, nxt, :, bottom], rb1.at[c, 2], right),
            ring(k + 3, part.at[c, prv, :, top], rb1.at[c, 3], left_id),
        ])

    def add2(a, b):
        return a.astype(F32) + b.astype(F32)

    def add3(a, b, c):
        return a.astype(F32) + b.astype(F32) + c.astype(F32)

    for c in range(2):
        pos, right, left_id = ring_ids(c)
        nxt, prv = (pos + 1) % 4, (pos + 3) % 4
        k = 6 * c
        phase1[c][0].wait_recv()
        for y in range(4):
            st1[c, 0, y] = add2(rb1[c, 0, y], part[c, nxt, y, 0:HALF]).astype(BF16)
        phase1[c].append(ring(k + 4, st1.at[c, 0], rb1.at[c, 4], right))
        phase1[c][1].wait_recv()
        for y in range(4):
            st1[c, 1, y] = add2(rb1[c, 1, y], part[c, prv, y, HALF:ROWS]).astype(BF16)
        phase1[c].append(ring(k + 5, st1.at[c, 1], rb1.at[c, 5], left_id))

    @pl.when(is_gowner)
    def _():
        wait_bytes(gall.at[pl.ds(0, 240)], gag_r.at[0])

    @pl.when(jnp.logical_not(is_gowner))
    def _():
        wait_bytes(gall.at[pl.ds(0, 256)], gag_r.at[0])

    def quarter(i):
        return gall.at[pl.ds(pl.multiple_of(256 * i, 256), 256)]

    lane_t = t % 2
    sibling = t + 1 - 2 * lane_t
    hop = (2 * h + t // 2 + 1 + 2 * lane_t) % 4
    gx = [
        copy_to(quarter(t), quarter(t), gx_s.at[0], gx_r.at[0],
                z * 8 + x * 2 + hop // 2, 2 * (hop % 2) + lane_t),
        copy_to(quarter(t), quarter(t), gx_s.at[1], gx_r.at[1], s, sibling),
    ]
    for g in gx:
        g.start()

    phase2 = []
    for c in range(2):
        pos, right, left_id = ring_ids(c)
        for cp in phase1[c][2:]:
            cp.wait_recv()
        for y in range(4):
            r1[c, y, 0:HALF] = add3(part[c, pos, y, 0:HALF], rb1[c, 4, y], rb1[c, 3, y]).astype(BF16)
            r1[c, y, HALF:ROWS] = add3(part[c, pos, y, HALF:ROWS], rb1[c, 5, y], rb1[c, 2, y]).astype(BF16)
        pos, right, left_id = ring_ids(1 - c)
        far, nxt, prv = (pos + 2) % 4, (pos + 1) % 4, (pos + 3) % 4
        k = 12 + 6 * c
        phase2.append([
            ring(k + 0, r1.at[c, far, top], rb2.at[c, 0], right),
            ring(k + 1, r1.at[c, far, bottom], rb2.at[c, 1], left_id),
            ring(k + 2, r1.at[c, nxt, bottom], rb2.at[c, 2], right),
            ring(k + 3, r1.at[c, prv, top], rb2.at[c, 3], left_id),
        ])
    gx[0].wait_recv()
    gx.append(copy_to(quarter(across), quarter(across), gx_s.at[2], gx_r.at[2], s, sibling))
    gx[2].start()
    for c in range(2):
        pos, right, left_id = ring_ids(1 - c)
        nxt, prv = (pos + 1) % 4, (pos + 3) % 4
        k = 12 + 6 * c
        phase2[c][0].wait_recv()
        st2[c, 0] = add2(rb2[c, 0], r1[c, nxt, 0:HALF]).astype(BF16)
        phase2[c].append(ring(k + 4, st2.at[c, 0], rb2.at[c, 4], right))
        phase2[c][1].wait_recv()
        st2[c, 1] = add2(rb2[c, 1], r1[c, prv, HALF:ROWS]).astype(BF16)
        phase2[c].append(ring(k + 5, st2.at[c, 1], rb2.at[c, 5], left_id))
    for c in range(2):
        pos, right, left_id = ring_ids(1 - c)
        for cp in phase2[c][2:]:
            cp.wait_recv()
        r2[c, 0:HALF] = add3(r1[c, pos, 0:HALF], rb2[c, 4], rb2[c, 3]).astype(BF16)
        r2[c, HALF:ROWS] = add3(r1[c, pos, HALF:ROWS], rb2[c, 5], rb2[c, 2]).astype(BF16)

    hx = ring(24, r2.at[1 - h], r3, pair)
    hx.wait_recv()
    ag[pl.ds(pl.multiple_of(ROWS * o, ROWS), ROWS), :] = add2(r2[h], r3[...]).astype(BF16)

    def piece(axis, first, second, k):
        zz, xx = (second, first) if axis == 0 else (first, second)
        return ag.at[pl.ds(pl.multiple_of(ROWS * (4 * zz + xx) + HALF * k, HALF), HALF)]

    def cols(ref, side):
        return ref.at[:, pl.ds(384 * side, 384)]

    lines = []
    for k in range(2):
        pa, ra, la = ring_ids(k)
        pb, rb, lb = ring_ids(1 - k)
        base = 25 + 16 * k
        own = piece(k, pa, pb, k)
        lines.append({"a": [ring(base, own, own, ra), ring(base + 1, own, own, la)], "r": [], "l": []})

    def send_b(k, n, first):
        pb, rb, lb = ring_ids(1 - k)
        base = 25 + 16 * k
        p = piece(k, first, pb, k)
        lines[k]["r"].append(ring(base + 4 + n, p, p, rb))
        lines[k]["l"].append(ring(base + 8 + n, p, p, lb))

    for k in range(2):
        send_b(k, 0, ring_ids(k)[0])
    for k in range(2):
        pa, ra, la = ring_ids(k)
        pb = ring_ids(1 - k)[0]
        base = 25 + 16 * k
        lines[k]["a"][0].wait_recv()
        p = cols(piece(k, (pa + 3) % 4, pb, k), 0)
        lines[k]["a"].append(ring(base + 2, p, p, ra))
        lines[k]["a"][1].wait_recv()
        p = cols(piece(k, (pa + 1) % 4, pb, k), 1)
        lines[k]["a"].append(ring(base + 3, p, p, la))
    for k in range(2):
        pa = ring_ids(k)[0]
        send_b(k, 1, (pa + 3) % 4)
        send_b(k, 2, (pa + 1) % 4)
    for k in range(2):
        pa = ring_ids(k)[0]
        lines[k]["a"][2].wait_recv()
        lines[k]["a"][3].wait_recv()
        send_b(k, 3, (pa + 2) % 4)
    order = (0, 3, 1, 2)
    for n in range(2):
        for k in range(2):
            pa = ring_ids(k)[0]
            pb, rb, lb = ring_ids(1 - k)
            base = 25 + 16 * k
            lines[k]["r"][n].wait_recv()
            p = piece(k, (pa + order[n]) % 4, (pb + 3) % 4, k)
            lines[k]["a"].append(ring(base + 12 + n, p, p, rb))

    gx[1].wait_recv()
    gx[2].wait_recv()
    eye = lax.broadcasted_iota(jnp.int32, (128, 128), 0) == lax.broadcasted_iota(jnp.int32, (128, 128), 1)

    def unpack(src, dst, tiles, band, double):
        bands = band // 128
        column = lax.broadcasted_iota(jnp.int32, (1, band), 1) // 128
        weight = jnp.where(jnp.logical_and(column > 0, column <= double), 2.0, 1.0)

        def body(i, carry):
            square, trace = carry
            at = pl.multiple_of(128 * i, 128)
            strip = src[pl.ds(at, 128), :]
            wide = strip.astype(F32)
            square = square + fold_rows(wide * wide) * weight
            trace = trace + fold_rows(jnp.where(eye, wide[:, 0:128], 0.0))
            for k in range(bands):
                to = pl.multiple_of(128 * ((i + k) % tiles), 128)
                dst[pl.ds(at, 128), pl.ds(to, 128)] = strip[:, 128 * k:128 * k + 128]
                if 1 <= k <= double:
                    dst[pl.ds(to, 128), pl.ds(at, 128)] = wide[:, 128 * k:128 * k + 128].T.astype(BF16)
            return square, trace

        square, trace = lax.fori_loop(
            0, tiles, body, (jnp.zeros((8, band), F32), jnp.zeros((8, 128), F32)))
        return total(square), total(trace)

    def norms(square, trace, width):
        shift = DAMPING * trace / width
        return shift, 1.0 / jnp.sqrt(square + 2.0 * shift * trace + shift * shift * width)

    @pl.when(active)
    def _():
        square, trace = unpack(gall, gfull, GT, GBAND, 3)
        shift, inv = norms(square, trace, float(DOUT))
        wait_bytes(wc.at[pl.ds(0, 31 * 32)], wa_r.at[0])
        y0 = wc[...].astype(F32)
        y1 = (dot(gfull[...], wc[...]) + shift * y0) * inv
        left[...] = y1.astype(BF16)
        y2 = (dot(gfull[...], left[...]) + shift * y1) * inv
        left[...] = y2.astype(BF16)
        y3 = (dot(gfull[...], left[...]) + shift * y2) * inv
        left[...] = (4.0 * y0 - 6.0 * y1 + 4.0 * y2 - y3).astype(BF16)
        vt[o] = left[pl.ds(pl.multiple_of(64 * o, 64), 64), :]

        @pl.loop(0, 16)
        def _(i):
            @pl.when(i != o)
            def _():
                copy_to(left.at[pl.ds(pl.multiple_of(64 * i, 64), 64)], vt.at[o],
                        lf_s.at[i], lf_r.at[0], 2 * i + h).start()

    for n in range(2, 4):
        for k in range(2):
            pa = ring_ids(k)[0]
            pb, rb, lb = ring_ids(1 - k)
            base = 25 + 16 * k
            lines[k]["l"][n].wait_recv()
            p = piece(k, (pa + order[n]) % 4, (pb + 1) % 4, k)
            lines[k]["a"].append(ring(base + 12 + n, p, p, lb))
    for k in range(2):
        for n in range(2, 4):
            lines[k]["r"][n].wait_recv()
        for n in range(2):
            lines[k]["l"][n].wait_recv()
        for cp in lines[k]["a"][4:]:
            cp.wait_recv()

    square, trace = unpack(ag, sfull, NT, BAND, 5)
    shift, inv = norms(square, trace, float(ABLK))

    @pl.when(active)
    def _():
        wait_bytes(vt.at[pl.ds(0, NT - 1)], lf_r.at[0])

    @pl.when(jnp.logical_not(active))
    def _():
        wait_bytes(vt, lf_r.at[0])

    for j in range(NT):
        vfull[:, 128 * j:128 * j + 128] = vt[j]
    y0 = vfull[...].astype(F32)
    y1 = (dot(vfull[...], sfull[...]) + shift * y0) * inv
    vfull[...] = y1.astype(BF16)
    upd[...] = 4.0 * y0 - 6.0 * y1
    y2 = (dot(vfull[...], sfull[...]) + shift * y1) * inv
    vfull[...] = y2.astype(BF16)
    upd[...] = upd[...] + 4.0 * y2
    y3 = (dot(vfull[...], sfull[...]) + shift * y2) * inv
    upd[...] = upd[...] - y3

    u_copy = copy_to(upd.at[pl.ds(pl.multiple_of(32 * (1 - h), 32), 32)], ux, one_s.at[1], one_r.at[1], pair)
    u_copy.start()

    wp_copy.wait_recv()
    acc = jnp.zeros((64, 128), F32)
    for j in range(NT):
        acc = acc + upd[:, 128 * j:128 * j + 128] * wpair[j].astype(F32)
    al[0] = fold_rows(acc)
    al1[t] = al[0]
    sums = []
    for d in range(1, 4):
        g = copy_to(al.at[0], al1.at[t], a1_s.at[d], a1_r.at[d], s, (t + d) % 4)
        g.start()
        sums.append(g)
    for g in sums:
        g.wait_recv()
    al[1] = (al1[0] + al1[1]) + (al1[2] + al1[3])
    al2[s] = al[1]

    @pl.loop(0, 32)
    def _(i):
        @pl.when(i != s)
        def _():
            copy_to(al.at[1], al2.at[s], a2_s.at[i], a2_r.at[0], i).start()

    u_copy.wait_recv()
    own = upd[pl.ds(pl.multiple_of(32 * h, 32), 32), :]
    other = ux[...]
    b0 = jnp.where(h == 0, own, other)
    b1 = jnp.where(h == 0, other, own)
    upd_out[:, 0:SPLIT] = b0[:, 0:SPLIT]
    upd_out[:, SPLIT:WIDTH] = jnp.where(lane < EDGE, b0[:, SPLIT:WIDTH], b1[:, SPLIT:WIDTH])
    upd_out[:, WIDTH:2688] = b1[:, 0:SPLIT]
    upd_out[:, 2688:2736] = b1[:, SPLIT:SPLIT + TAIL]

    wait_bytes(al2.at[pl.ds(0, 31)], a2_r.at[0])
    acc = al2[0]
    for i in range(1, 32):
        acc = acc + al2[i]
    ratio = jnp.minimum(1.0, CLIP_LEVEL / jnp.sqrt(total(acc) / (DOUT * FF)))
    upd_out[...] = upd_out[...] * ratio

    for cp in pending + gx + sums + [wp_copy, u_copy]:
        cp.wait_send()

    @pl.loop(0, 16)
    def _(i):
        @pl.when(2 * i + g_lane != s)
        def _():
            wait_bytes(gq.at[pl.ds(0, GROWS)], grs_s.at[i])

        @pl.when(jnp.logical_and(active, i != o))
        def _():
            wait_bytes(left.at[pl.ds(0, 64)], lf_s.at[i])

    for b in range(2):
        @pl.loop(0, NT)
        def _(j):
            @pl.when(2 * j + b != s)
            def _():
                wait_bytes(w2.at[b, j], wa_s.at[b * NT + j])

    @pl.loop(0, 32)
    def _(i):
        @pl.when(i != s)
        def _():
            wait_bytes(al.at[1], a2_s.at[i])

        @pl.when(jnp.logical_and(is_gowner, i != s))
        def _():
            wait_bytes(gall.at[pl.ds(0, GROWS)], gag_s.at[i])


def whole_step(sample_idx, out_grads, grad_weight, hidden_acts):
    dma = pltpu.SemaphoreType.DMA
    vmem = pltpu.VMEM
    return pl.pallas_call(
        kernel,
        out_shape=jax.ShapeDtypeStruct((MINE, 2 * ABLK), F32),
        in_specs=[pl.BlockSpec(memory_space=pltpu.VMEM)] + [pl.BlockSpec(memory_space=pl.ANY)] * 3,
        out_specs=pl.BlockSpec(memory_space=pltpu.VMEM),
        scratch_shapes=[
            vmem((2, 256, DOUT), BF16),
            vmem((MINE, 2 * ABLK), BF16),
            vmem((2, 2 * ABLK, 256), BF16),
            vmem((2, WIDTH + 640, 256), BF16),
            vmem((256, DOUT + 512), BF16),
            vmem((2, 4, 4, ROWS, BAND), BF16),
            vmem((2, NT, 32, 128), BF16),
            vmem((NT, 64, 128), BF16),
            vmem((DOUT, 128), BF16),
            vmem((128, 256), F32),
            vmem((256, GBAND), BF16),
            vmem((32, GROWS, GBAND), BF16),
            vmem((DOUT, GBAND), BF16),
            vmem((DOUT, DOUT), BF16),
            vmem((2, 6, 4, HALF, BAND), BF16),
            vmem((2, 2, 4, HALF, BAND), BF16),
            vmem((2, 4, ROWS, BAND), BF16),
            vmem((2, 6, HALF, BAND), BF16),
            vmem((2, 2, HALF, BAND), BF16),
            vmem((2, ROWS, BAND), BF16),
            vmem((ROWS, BAND), BF16),
            vmem((16 * ROWS, BAND), BF16),
            vmem((WIDTH, WIDTH), BF16),
            vmem((NT, 64, 128), BF16),
            vmem((64, WIDTH), BF16),
            vmem((DOUT, 128), BF16),
            vmem((64, WIDTH), F32),
            vmem((32, WIDTH), F32),
            vmem((2, 8, 128), F32),
            vmem((4, 8, 128), F32),
            vmem((32, 8, 128), F32),
            dma((16,)), dma((1,)),
            dma((32,)), dma((1,)),
            dma((4,)), dma((4,)),
            dma((2 * NT,)), dma((1,)),
            dma((16,)), dma((1,)),
            dma((57,)), dma((57,)),
            dma((4,)), dma((4,)),
            dma((32,)), dma((1,)),
            dma((2,)), dma((2,)), dma((3,)),
        ],
        compiler_params=pltpu.CompilerParams(
            collective_id=0, has_side_effects=True, vmem_limit_bytes=60 * 1024 * 1024),
    )(sample_idx, out_grads, grad_weight, hidden_acts)


def per_device(hidden_acts, out_grads, sample_idx, grad_weight, momentum, weight):
    scaled = whole_step(sample_idx, out_grads, grad_weight, jnp.swapaxes(hidden_acts, 1, 2))
    new_momentum = MOMENTUM_RATE * momentum + scaled
    new_weight = weight - LEARN_RATE * new_momentum
    return (new_momentum, new_weight)


def solution(mesh):
    in_specs = (
        P(None, "shard", "tensor"),
        P(None, "shard", None),
        P(None, "shard"),
        P("shard", "tensor"),
        P("shard", "tensor"),
        P("shard", "tensor"),
    )
    out_specs = (P("shard", "tensor"), P("shard", "tensor"))
    return jax.shard_map(
        per_device, mesh=mesh, in_specs=in_specs, out_specs=out_specs, check_vma=False
    )
```

```python
import jax
import jax.numpy as jnp
from jax import lax
from jax.experimental import pallas as pl
from jax.experimental.pallas import tpu as pltpu
from jax.sharding import PartitionSpec as P

DOUT = 1024
FF = 10944
ABLK = 1368
DAMPING = 0.1
CLIP_LEVEL = 0.5
MOMENTUM_RATE = 0.9
LEARN_RATE = 0.5

F32 = jnp.float32
BF16 = jnp.bfloat16
MESH = pl.DeviceIdType.MESH

NT = 11
WIDTH = NT * 128
SPLIT = 1280
EDGE = ABLK - SPLIT
TAIL = 2 * ABLK - 2688
BAND = 6 * 128
ROWS = 96
HALF = ROWS // 2
GT = DOUT // 128
GBAND = 5 * 128
GROWS = 16
MINE = 32


def dot(a, b):
    return lax.dot_general(a, b, (((1,), (0,)), ((), ())), preferred_element_type=F32)


def dot_tn(a, b):
    return lax.dot_general(a, b, (((0,), (0,)), ((), ())), preferred_element_type=F32)


def fold_rows(value):
    return value.reshape(value.shape[0] // 8, 8, value.shape[1]).sum(0)


def dot_nt(a, b):
    return lax.dot_general(a, b, (((1,), (1,)), ((), ())), preferred_element_type=F32)


def total(value):
    return jnp.sum(jnp.sum(value, axis=1, keepdims=True), axis=0, keepdims=True)


def kernel(
    idx_ref, grads_hbm, w_hbm, acts_hbm,
    upd_out,
    grads_ref, w_ref, acts_ref,
    picked, gpicked, part, w2, wpair, wc, edge,
    gq, grecv, gall, gfull,
    rb1, st1, r1, rb2, st2, r2, r3,
    ag, sfull, vt, vfull, left, upd, ub, ux, al, al1, al2,
    grs_s, grs_r, gag_s, gag_r, gx_s, gx_r, wa_s, wa_r, lf_s, lf_r,
    ring_s, ring_r, a1_s, a1_r, a2_s, a2_r, one_s, one_r, in_s,
):
    s = lax.axis_index("shard")
    t = lax.axis_index("tensor")
    z, x, h, o = s // 8, (s // 2) % 4, s % 2, s // 2
    pair = o * 2 + (1 - h)
    scale = 1.0 / 8192.0
    lane = lax.broadcasted_iota(jnp.int32, (1, 128), 1)

    def copy_to(src, dst, send, recv, shard, tensor=None):
        return pltpu.make_async_remote_copy(
            src_ref=src, dst_ref=dst, send_sem=send, recv_sem=recv,
            device_id=(shard, t if tensor is None else tensor), device_id_type=MESH,
        )

    def wait_bytes(ref, sem):
        pltpu.make_async_copy(ref, ref, sem).wait()

    loads = [
        pltpu.make_async_copy(grads_hbm, grads_ref, in_s.at[0]),
        pltpu.make_async_copy(w_hbm, w_ref, in_s.at[1]),
        pltpu.make_async_copy(acts_hbm, acts_ref, in_s.at[2]),
    ]
    for load in loads:
        load.start()

    barrier = pltpu.get_barrier_semaphore()

    @pl.loop(0, 32)
    def _(i):
        @pl.when(i != s)
        def _():
            pl.semaphore_signal(barrier, inc=1, device_id=(i, t), device_id_type=MESH)

    for d in range(1, 4):
        pl.semaphore_signal(barrier, inc=1, device_id=(s, (t + d) % 4), device_id_type=MESH)
        pl.semaphore_signal(barrier, inc=1, device_id=(pair, (t + d) % 4), device_id_type=MESH)

    is_gowner = h == t % 2
    sibling = t + 1 - 2 * (t % 2)
    along = 2 * h + t // 2

    def chip(step):
        there = (along + step) % 4
        return z * 8 + x * 2 + there // 2, 2 * (there % 2) + there // 2

    @pl.when(is_gowner)
    def _():
        pl.semaphore_signal(barrier, inc=1, device_id=chip(1), device_id_type=MESH)
        pl.semaphore_signal(barrier, inc=1, device_id=chip(3), device_id_type=MESH)


    hots = []
    for m in range(2):
        token = lax.broadcasted_iota(jnp.int32, (256, 128), 0)
        hots.append(jnp.where(token == idx_ref[m:m + 1, :], 1.0, 0.0).astype(BF16))
    loads[0].wait()
    for m in range(2):
        rows = slice(128 * m, 128 * m + 128)
        pg = dot_tn(hots[m], grads_ref[m]).astype(BF16)
        gpicked[rows, 0:DOUT] = pg
        gpicked[rows, DOUT:DOUT + 512] = pg[:, 0:512]
    for i in range(2):
        at = pl.multiple_of(128 * (2 * t + i), 128)
        strip = dot_tn(gpicked[:, pl.ds(at, 128)], gpicked[:, pl.ds(at, GBAND)])
        gq[128 * i:128 * i + 128, :] = (strip * scale).astype(BF16)

    loads[1].wait()
    for j in range(NT - 1):
        w2[0, j] = w_ref[:, 128 * j:128 * j + 128]
        w2[1, j] = w_ref[:, WIDTH + 128 * j:WIDTH + 128 * j + 128]
    cut = w_ref[:, SPLIT:WIDTH].astype(F32)
    w2[0, NT - 1] = jnp.where(lane < EDGE, cut, 0.0).astype(BF16)
    edge[0:32, 0:128] = jnp.where(lane >= EDGE, cut, 0.0)
    edge[0:32, 0:TAIL] = w_ref[:, 2688:2736].astype(F32)
    w2[1, NT - 1] = edge[0:32, 0:128].astype(BF16)
    wpair[:, pl.ds(pl.multiple_of(32 * h, 32), 32), :] = w2[h]

    @pl.when(is_gowner)
    def _():
        pl.semaphore_wait(barrier, 39)

    @pl.when(jnp.logical_not(is_gowner))
    def _():
        pl.semaphore_wait(barrier, 37)


    g_lane = t % 2

    @pl.loop(0, 16)
    def _(i):
        to = 2 * i + g_lane

        @pl.when(to != s)
        def _():
            copy_to(gq.at[pl.ds(pl.multiple_of(GROWS * i, GROWS), GROWS)], grecv.at[s],
                    grs_s.at[i], grs_r.at[0], to).start()

    for b in range(2):
        @pl.loop(0, NT)
        def _(j):
            to = 2 * j + b

            @pl.when(to != s)
            def _():
                copy_to(w2.at[b, j], wc.at[pl.ds(pl.multiple_of(32 * s, 32), 32)],
                        wa_s.at[b * NT + j], wa_r.at[0], to).start()

    active = o < NT

    @pl.when(active)
    def _():
        wc[pl.ds(pl.multiple_of(32 * s, 32), 32), :] = w2[h, jnp.minimum(o, NT - 1)]

    wp_copy = copy_to(w2.at[1 - h], wpair.at[:, pl.ds(pl.multiple_of(32 * h, 32), 32), :],
                      one_s.at[0], one_r.at[0], pair)
    wp_copy.start()

    @pl.when(is_gowner)
    def _():
        grecv[s] = gq[pl.ds(pl.multiple_of(GROWS * o, GROWS), GROWS), :]

    def ring_ids(axis):
        if axis == 0:
            return x, z * 8 + ((x + 1) % 4) * 2 + h, z * 8 + ((x + 3) % 4) * 2 + h
        return z, ((z + 1) % 4) * 8 + x * 2 + h, ((z + 3) % 4) * 8 + x * 2 + h

    part[0, 2, 3, 64:96] = jnp.zeros((32, BAND), BF16)
    part[0, 3, 3] = jnp.zeros((96, BAND), BF16)
    part[1, 3, 2, 64:96] = jnp.zeros((32, BAND), BF16)
    part[1, 3, 3] = jnp.zeros((96, BAND), BF16)

    pending = []
    loads[2].wait()
    high = lax.broadcasted_iota(jnp.int32, (128, 1), 0) >= EDGE

    def ring(k, src, dst, to):
        c = copy_to(src, dst, ring_s.at[k], ring_r.at[k], to)
        c.start()
        pending.append(c)
        return c

    phase1 = []
    for c in range(2):
        for m in range(2):
            cols_m = slice(128 * m, 128 * m + 128)
            if c == 0:
                pa = dot(acts_ref[m, 0:WIDTH, :], hots[m])
                picked[c, 0:SPLIT, cols_m] = pa[0:SPLIT].astype(BF16)
                cut = pa[SPLIT:WIDTH]
                picked[c, SPLIT:WIDTH, cols_m] = jnp.where(high, 0.0, cut).astype(BF16)
                edge[:, cols_m] = jnp.where(high, cut, 0.0)
            else:
                pa = dot(acts_ref[m, WIDTH:2 * ABLK, :], hots[m])
                picked[c, 0:SPLIT, cols_m] = pa[0:SPLIT].astype(BF16)
                edge[0:TAIL, cols_m] = pa[SPLIT:SPLIT + TAIL]
                picked[c, SPLIT:WIDTH, cols_m] = edge[:, cols_m].astype(BF16)
        picked[c, WIDTH:WIDTH + 640, :] = picked[c, 0:640, :]

        @pl.loop(0, NT)
        def _(i):
            at = pl.multiple_of(128 * i, 128)
            strip = dot_nt(picked[c, pl.ds(at, 128), :], picked[c, pl.ds(at, BAND), :])
            strip = (strip * scale).astype(BF16)
            for q in range(4):
                u = 4 * i + q
                oo = u // 3
                row = pl.multiple_of((u % 3) * 32, 32)
                zz, xx = oo // 4, oo % 4
                piece = strip[32 * q:32 * q + 32]
                if c == 0:
                    part[0, xx, zz, pl.ds(row, 32), :] = piece
                else:
                    part[1, zz, xx, pl.ds(row, 32), :] = piece

        if c == 0:
            @pl.when(is_gowner)
            def _():
                wait_bytes(grecv.at[pl.ds(0, 31)], grs_r.at[0])
                acc = grecv[0].astype(F32)
                for i in range(1, 32):
                    acc = acc + grecv[i].astype(F32)
                gall[pl.ds(pl.multiple_of(256 * t + GROWS * o, GROWS), GROWS), :] = acc.astype(BF16)

                @pl.loop(0, 16)
                def _(i):
                    @pl.when(i != o)
                    def _():
                        mine = gall.at[pl.ds(pl.multiple_of(256 * t + GROWS * o, GROWS), GROWS)]
                        copy_to(mine, mine, gag_s.at[i], gag_r.at[0], 2 * i + h).start()

        pos, right, left_id = ring_ids(c)
        far, nxt, prv = (pos + 2) % 4, (pos + 1) % 4, (pos + 3) % 4
        k = 6 * c
        top, bottom = pl.ds(0, HALF), pl.ds(HALF, HALF)
        phase1.append([
            ring(k + 0, part.at[c, far, :, top], rb1.at[c, 0], right),
            ring(k + 1, part.at[c, far, :, bottom], rb1.at[c, 1], left_id),
            ring(k + 2, part.at[c, nxt, :, bottom], rb1.at[c, 2], right),
            ring(k + 3, part.at[c, prv, :, top], rb1.at[c, 3], left_id),
        ])

    def add2(a, b):
        return a.astype(F32) + b.astype(F32)

    def add3(a, b, c):
        return a.astype(F32) + b.astype(F32) + c.astype(F32)

    def quarter(step):
        return gall.at[pl.ds(pl.multiple_of(256 * chip(step)[1], 256), 256)]

    def half_quarter(step, side):
        return gall.at[pl.ds(pl.multiple_of(256 * chip(step)[1] + 128 * side, 128), 128)]

    def along_y(k, ref, to):
        copy_to(ref, ref, gx_s.at[k], gx_r.at[k], *to).start()

    @pl.when(is_gowner)
    def _():
        wait_bytes(gall.at[pl.ds(0, 240)], gag_r.at[0])
        along_y(0, quarter(0), chip(1))
        along_y(1, quarter(0), chip(3))
        along_y(2, quarter(0), (s, sibling))

    for c in range(2):
        pos, right, left_id = ring_ids(c)
        nxt, prv = (pos + 1) % 4, (pos + 3) % 4
        k = 6 * c
        phase1[c][0].wait_recv()
        for y in range(4):
            st1[c, 0, y] = add2(rb1[c, 0, y], part[c, nxt, y, 0:HALF]).astype(BF16)
        phase1[c].append(ring(k + 4, st1.at[c, 0], rb1.at[c, 4], right))
        phase1[c][1].wait_recv()
        for y in range(4):
            st1[c, 1, y] = add2(rb1[c, 1, y], part[c, prv, y, HALF:ROWS]).astype(BF16)
        phase1[c].append(ring(k + 5, st1.at[c, 1], rb1.at[c, 5], left_id))

    phase2 = []
    for c in range(2):
        pos, right, left_id = ring_ids(c)
        for cp in phase1[c][2:]:
            cp.wait_recv()
        for y in range(4):
            r1[c, y, 0:HALF] = add3(part[c, pos, y, 0:HALF], rb1[c, 4, y], rb1[c, 3, y]).astype(BF16)
            r1[c, y, HALF:ROWS] = add3(part[c, pos, y, HALF:ROWS], rb1[c, 5, y], rb1[c, 2, y]).astype(BF16)
        pos, right, left_id = ring_ids(1 - c)
        far, nxt, prv = (pos + 2) % 4, (pos + 1) % 4, (pos + 3) % 4
        k = 12 + 6 * c
        phase2.append([
            ring(k + 0, r1.at[c, far, top], rb2.at[c, 0], right),
            ring(k + 1, r1.at[c, far, bottom], rb2.at[c, 1], left_id),
            ring(k + 2, r1.at[c, nxt, bottom], rb2.at[c, 2], right),
            ring(k + 3, r1.at[c, prv, top], rb2.at[c, 3], left_id),
        ])
    @pl.when(is_gowner)
    def _():
        wait_bytes(quarter(3), gx_r.at[0])
        along_y(3, half_quarter(3, 0), chip(1))
        along_y(5, quarter(3), (s, sibling))
        wait_bytes(quarter(1), gx_r.at[1])
        along_y(4, half_quarter(1, 1), chip(3))
        along_y(6, quarter(1), (s, sibling))
        wait_bytes(half_quarter(2, 0), gx_r.at[3])
        wait_bytes(half_quarter(2, 1), gx_r.at[4])
        along_y(7, quarter(2), (s, sibling))

    for c in range(2):
        pos, right, left_id = ring_ids(1 - c)
        nxt, prv = (pos + 1) % 4, (pos + 3) % 4
        k = 12 + 6 * c
        phase2[c][0].wait_recv()
        st2[c, 0] = add2(rb2[c, 0], r1[c, nxt, 0:HALF]).astype(BF16)
        phase2[c].append(ring(k + 4, st2.at[c, 0], rb2.at[c, 4], right))
        phase2[c][1].wait_recv()
        st2[c, 1] = add2(rb2[c, 1], r1[c, prv, HALF:ROWS]).astype(BF16)
        phase2[c].append(ring(k + 5, st2.at[c, 1], rb2.at[c, 5], left_id))
    @pl.when(jnp.logical_not(is_gowner))
    def _():
        for k in (2, 5, 6, 7):
            wait_bytes(gall.at[pl.ds(0, 256)], gx_r.at[k])

    eye = lax.broadcasted_iota(jnp.int32, (128, 128), 0) == lax.broadcasted_iota(jnp.int32, (128, 128), 1)

    def unpack(src, dst, tiles, band, double):
        bands = band // 128
        column = lax.broadcasted_iota(jnp.int32, (1, band), 1) // 128
        weight = jnp.where(jnp.logical_and(column > 0, column <= double), 2.0, 1.0)

        def body(i, carry):
            square, trace = carry
            at = pl.multiple_of(128 * i, 128)
            strip = src[pl.ds(at, 128), :]
            wide = strip.astype(F32)
            square = square + fold_rows(wide * wide) * weight
            trace = trace + fold_rows(jnp.where(eye, wide[:, 0:128], 0.0))
            for k in range(bands):
                to = pl.multiple_of(128 * ((i + k) % tiles), 128)
                dst[pl.ds(at, 128), pl.ds(to, 128)] = strip[:, 128 * k:128 * k + 128]
                if 1 <= k <= double:
                    dst[pl.ds(to, 128), pl.ds(at, 128)] = wide[:, 128 * k:128 * k + 128].T.astype(BF16)
            return square, trace

        square, trace = lax.fori_loop(
            0, tiles, body, (jnp.zeros((8, band), F32), jnp.zeros((8, 128), F32)))
        return total(square), total(trace)

    def norms(square, trace, width):
        shift = DAMPING * trace / width
        return shift, 1.0 / jnp.sqrt(square + 2.0 * shift * trace + shift * shift * width)

    @pl.when(active)
    def _():
        square, trace = unpack(gall, gfull, GT, GBAND, 3)
        shift, inv = norms(square, trace, float(DOUT))
        wait_bytes(wc.at[pl.ds(0, 31 * 32)], wa_r.at[0])
        y0 = wc[...].astype(F32)
        y1 = (dot(gfull[...], wc[...]) + shift * y0) * inv
        left[...] = y1.astype(BF16)
        y2 = (dot(gfull[...], left[...]) + shift * y1) * inv
        left[...] = y2.astype(BF16)
        y3 = (dot(gfull[...], left[...]) + shift * y2) * inv
        left[...] = (4.0 * y0 - 6.0 * y1 + 4.0 * y2 - y3).astype(BF16)
        vt[o] = left[pl.ds(pl.multiple_of(64 * o, 64), 64), :]

        @pl.loop(0, 16)
        def _(i):
            @pl.when(i != o)
            def _():
                copy_to(left.at[pl.ds(pl.multiple_of(64 * i, 64), 64)], vt.at[o],
                        lf_s.at[i], lf_r.at[0], 2 * i + h).start()

    for c in range(2):
        pos, right, left_id = ring_ids(1 - c)
        for cp in phase2[c][2:]:
            cp.wait_recv()
        r2[c, 0:HALF] = add3(r1[c, pos, 0:HALF], rb2[c, 4], rb2[c, 3]).astype(BF16)
        r2[c, HALF:ROWS] = add3(r1[c, pos, HALF:ROWS], rb2[c, 5], rb2[c, 2]).astype(BF16)

    hx = ring(24, r2.at[1 - h], r3, pair)
    hx.wait_recv()
    ag[pl.ds(pl.multiple_of(ROWS * o, ROWS), ROWS), :] = add2(r2[h], r3[...]).astype(BF16)

    def piece(axis, first, second, k):
        zz, xx = (second, first) if axis == 0 else (first, second)
        return ag.at[pl.ds(pl.multiple_of(ROWS * (4 * zz + xx) + HALF * k, HALF), HALF)]

    def cols(ref, side):
        return ref.at[:, pl.ds(384 * side, 384)]

    lines = []
    for k in range(2):
        pa, ra, la = ring_ids(k)
        pb, rb, lb = ring_ids(1 - k)
        base = 25 + 16 * k
        own = piece(k, pa, pb, k)
        lines.append({"a": [ring(base, own, own, ra), ring(base + 1, own, own, la)], "r": [], "l": []})

    def send_b(k, n, first):
        pb, rb, lb = ring_ids(1 - k)
        base = 25 + 16 * k
        p = piece(k, first, pb, k)
        lines[k]["r"].append(ring(base + 4 + n, p, p, rb))
        lines[k]["l"].append(ring(base + 8 + n, p, p, lb))

    for k in range(2):
        send_b(k, 0, ring_ids(k)[0])
    for k in range(2):
        pa, ra, la = ring_ids(k)
        pb = ring_ids(1 - k)[0]
        base = 25 + 16 * k
        lines[k]["a"][0].wait_recv()
        p = cols(piece(k, (pa + 3) % 4, pb, k), 0)
        lines[k]["a"].append(ring(base + 2, p, p, ra))
        lines[k]["a"][1].wait_recv()
        p = cols(piece(k, (pa + 1) % 4, pb, k), 1)
        lines[k]["a"].append(ring(base + 3, p, p, la))
    for k in range(2):
        pa = ring_ids(k)[0]
        send_b(k, 1, (pa + 3) % 4)
        send_b(k, 2, (pa + 1) % 4)
    for k in range(2):
        pa = ring_ids(k)[0]
        lines[k]["a"][2].wait_recv()
        lines[k]["a"][3].wait_recv()
        send_b(k, 3, (pa + 2) % 4)
    order = (0, 3, 1, 2)
    for n in range(2):
        for k in range(2):
            pa = ring_ids(k)[0]
            pb, rb, lb = ring_ids(1 - k)
            base = 25 + 16 * k
            lines[k]["r"][n].wait_recv()
            p = piece(k, (pa + order[n]) % 4, (pb + 3) % 4, k)
            lines[k]["a"].append(ring(base + 12 + n, p, p, rb))

    for n in range(2, 4):
        for k in range(2):
            pa = ring_ids(k)[0]
            pb, rb, lb = ring_ids(1 - k)
            base = 25 + 16 * k
            lines[k]["l"][n].wait_recv()
            p = piece(k, (pa + order[n]) % 4, (pb + 1) % 4, k)
            lines[k]["a"].append(ring(base + 12 + n, p, p, lb))
    for k in range(2):
        for n in range(2, 4):
            lines[k]["r"][n].wait_recv()
        for n in range(2):
            lines[k]["l"][n].wait_recv()
        for cp in lines[k]["a"][4:]:
            cp.wait_recv()

    square, trace = unpack(ag, sfull, NT, BAND, 5)
    shift, inv = norms(square, trace, float(ABLK))

    @pl.when(active)
    def _():
        wait_bytes(vt.at[pl.ds(0, NT - 1)], lf_r.at[0])

    @pl.when(jnp.logical_not(active))
    def _():
        wait_bytes(vt, lf_r.at[0])

    for j in range(NT):
        vfull[:, 128 * j:128 * j + 128] = vt[j]
    y0 = vfull[...].astype(F32)
    y1 = (dot(vfull[...], sfull[...]) + shift * y0) * inv
    vfull[...] = y1.astype(BF16)
    upd[...] = 4.0 * y0 - 6.0 * y1
    y2 = (dot(vfull[...], sfull[...]) + shift * y1) * inv
    vfull[...] = y2.astype(BF16)
    upd[...] = upd[...] + 4.0 * y2
    y3 = (dot(vfull[...], sfull[...]) + shift * y2) * inv
    upd[...] = upd[...] - y3

    wp_copy.wait_recv()
    acc = jnp.zeros((64, 128), F32)
    for j in range(NT):
        acc = acc + upd[:, 128 * j:128 * j + 128] * wpair[j].astype(F32)
    al[0] = fold_rows(acc)
    here = 4 * h + t
    al1[here] = al[0]
    sums = []
    for d in range(1, 8):
        there = (here + d) % 8
        g = copy_to(al.at[0], al1.at[here], a1_s.at[d], a1_r.at[d], 2 * o + there // 4, there % 4)
        g.start()
        sums.append(g)
    for g in sums:
        g.wait_recv()
    acc = al1[0]
    for i in range(1, 8):
        acc = acc + al1[i]
    al[1] = acc
    al2[o] = acc

    @pl.loop(0, 16)
    def _(i):
        @pl.when(i != o)
        def _():
            copy_to(al.at[1], al2.at[o], a2_s.at[i], a2_r.at[0], 2 * i + h).start()

    ub[...] = upd[pl.ds(pl.multiple_of(32 * (1 - h), 32), 32), :].astype(BF16)
    u_copy = copy_to(ub, ux, one_s.at[1], one_r.at[1], pair)
    u_copy.start()
    u_copy.wait_recv()
    own = upd[pl.ds(pl.multiple_of(32 * h, 32), 32), :]
    other = ux[...].astype(F32)
    b0 = jnp.where(h == 0, own, other)
    b1 = jnp.where(h == 0, other, own)
    upd_out[:, 0:SPLIT] = b0[:, 0:SPLIT]
    upd_out[:, SPLIT:WIDTH] = jnp.where(lane < EDGE, b0[:, SPLIT:WIDTH], b1[:, SPLIT:WIDTH])
    upd_out[:, WIDTH:2688] = b1[:, 0:SPLIT]
    upd_out[:, 2688:2736] = b1[:, SPLIT:SPLIT + TAIL]

    wait_bytes(al2.at[pl.ds(0, 15)], a2_r.at[0])
    acc = al2[0]
    for i in range(1, 16):
        acc = acc + al2[i]
    ratio = jnp.minimum(1.0, CLIP_LEVEL / jnp.sqrt(total(acc) / (DOUT * FF)))
    upd_out[...] = upd_out[...] * ratio

    for cp in pending + sums + [wp_copy, u_copy]:
        cp.wait_send()

    @pl.when(is_gowner)
    def _():
        for k in range(8):
            wait_bytes(gall.at[pl.ds(0, 128 if k in (3, 4) else 256)], gx_s.at[k])

    @pl.loop(0, 16)
    def _(i):
        @pl.when(2 * i + g_lane != s)
        def _():
            wait_bytes(gq.at[pl.ds(0, GROWS)], grs_s.at[i])

        @pl.when(jnp.logical_and(active, i != o))
        def _():
            wait_bytes(left.at[pl.ds(0, 64)], lf_s.at[i])

        @pl.when(i != o)
        def _():
            wait_bytes(al.at[1], a2_s.at[i])

        @pl.when(jnp.logical_and(is_gowner, i != o))
        def _():
            wait_bytes(gall.at[pl.ds(0, GROWS)], gag_s.at[i])

    for b in range(2):
        @pl.loop(0, NT)
        def _(j):
            @pl.when(2 * j + b != s)
            def _():
                wait_bytes(w2.at[b, j], wa_s.at[b * NT + j])


def whole_step(sample_idx, out_grads, grad_weight, hidden_acts):
    dma = pltpu.SemaphoreType.DMA
    vmem = pltpu.VMEM
    return pl.pallas_call(
        kernel,
        out_shape=jax.ShapeDtypeStruct((MINE, 2 * ABLK), F32),
        in_specs=[pl.BlockSpec(memory_space=pltpu.VMEM)] + [pl.BlockSpec(memory_space=pl.ANY)] * 3,
        out_specs=pl.BlockSpec(memory_space=pltpu.VMEM),
        scratch_shapes=[
            vmem((2, 256, DOUT), BF16),
            vmem((MINE, 2 * ABLK), BF16),
            vmem((2, 2 * ABLK, 256), BF16),
            vmem((2, WIDTH + 640, 256), BF16),
            vmem((256, DOUT + 512), BF16),
            vmem((2, 4, 4, ROWS, BAND), BF16),
            vmem((2, NT, 32, 128), BF16),
            vmem((NT, 64, 128), BF16),
            vmem((DOUT, 128), BF16),
            vmem((128, 256), F32),
            vmem((256, GBAND), BF16),
            vmem((32, GROWS, GBAND), BF16),
            vmem((DOUT, GBAND), BF16),
            vmem((DOUT, DOUT), BF16),
            vmem((2, 6, 4, HALF, BAND), BF16),
            vmem((2, 2, 4, HALF, BAND), BF16),
            vmem((2, 4, ROWS, BAND), BF16),
            vmem((2, 6, HALF, BAND), BF16),
            vmem((2, 2, HALF, BAND), BF16),
            vmem((2, ROWS, BAND), BF16),
            vmem((ROWS, BAND), BF16),
            vmem((16 * ROWS, BAND), BF16),
            vmem((WIDTH, WIDTH), BF16),
            vmem((NT, 64, 128), BF16),
            vmem((64, WIDTH), BF16),
            vmem((DOUT, 128), BF16),
            vmem((64, WIDTH), F32),
            vmem((32, WIDTH), BF16),
            vmem((32, WIDTH), BF16),
            vmem((2, 8, 128), F32),
            vmem((8, 8, 128), F32),
            vmem((16, 8, 128), F32),
            dma((16,)), dma((1,)),
            dma((16,)), dma((1,)),
            dma((8,)), dma((8,)),
            dma((2 * NT,)), dma((1,)),
            dma((16,)), dma((1,)),
            dma((57,)), dma((57,)),
            dma((8,)), dma((8,)),
            dma((16,)), dma((1,)),
            dma((2,)), dma((2,)), dma((3,)),
        ],
        compiler_params=pltpu.CompilerParams(
            collective_id=0, has_side_effects=True, vmem_limit_bytes=60 * 1024 * 1024),
    )(sample_idx, out_grads, grad_weight, hidden_acts)


def per_device(hidden_acts, out_grads, sample_idx, grad_weight, momentum, weight):
    scaled = whole_step(sample_idx, out_grads, grad_weight, jnp.swapaxes(hidden_acts, 1, 2))
    new_momentum = MOMENTUM_RATE * momentum + scaled
    new_weight = weight - LEARN_RATE * new_momentum
    return (new_momentum, new_weight)


def solution(mesh):
    in_specs = (
        P(None, "shard", "tensor"),
        P(None, "shard", None),
        P(None, "shard"),
        P("shard", "tensor"),
        P("shard", "tensor"),
        P("shard", "tensor"),
    )
    out_specs = (P("shard", "tensor"), P("shard", "tensor"))
    return jax.shard_map(
        per_device, mesh=mesh, in_specs=in_specs, out_specs=out_specs, check_vma=False
    )
```

```python
import jax
import jax.numpy as jnp
from jax import lax
from jax.experimental import pallas as pl
from jax.experimental.pallas import tpu as pltpu
from jax.sharding import PartitionSpec as P

DOUT = 1024
FF = 10944
ABLK = 1368
DAMPING = 0.1
CLIP_LEVEL = 0.5
MOMENTUM_RATE = 0.9
LEARN_RATE = 0.5

F32 = jnp.float32
BF16 = jnp.bfloat16
MESH = pl.DeviceIdType.MESH

NT = 11
WIDTH = NT * 128
SPLIT = 1280
EDGE = ABLK - SPLIT
TAIL = 2 * ABLK - 2688
BAND = 6 * 128
ROWS = 96
HALF = ROWS // 2
GT = DOUT // 128
GBAND = 5 * 128
GROWS = 16
MINE = 32


def dot(a, b):
    return lax.dot_general(a, b, (((1,), (0,)), ((), ())), preferred_element_type=F32)


def dot_tn(a, b):
    return lax.dot_general(a, b, (((0,), (0,)), ((), ())), preferred_element_type=F32)


def fold_rows(value):
    return value.reshape(value.shape[0] // 8, 8, value.shape[1]).sum(0)


def dot_nt(a, b):
    return lax.dot_general(a, b, (((1,), (1,)), ((), ())), preferred_element_type=F32)


def total(value):
    return jnp.sum(jnp.sum(value, axis=1, keepdims=True), axis=0, keepdims=True)


def kernel(
    idx_ref, grads_hbm, w_hbm, acts_hbm,
    upd_out,
    grads_ref, w_ref, acts_ref,
    picked, gpicked, part, w2, wpair, wc, edge,
    gq, grecv, gall, gfull,
    rb1, st1, r1, rb2, st2, r2, r3,
    ag, sfull, vt, vfull, left, upd, ub, ux, al, al1, al2,
    grs_s, grs_r, gag_s, gag_r, gx_s, gx_r, wa_s, wa_r, lf_s, lf_r,
    ring_s, ring_r, a1_s, a1_r, a2_s, a2_r, one_s, one_r, in_s,
):
    s = lax.axis_index("shard")
    t = lax.axis_index("tensor")
    z, x, h, o = s // 8, (s // 2) % 4, s % 2, s // 2
    pair = o * 2 + (1 - h)
    scale = 1.0 / 8192.0
    lane = lax.broadcasted_iota(jnp.int32, (1, 128), 1)

    def copy_to(src, dst, send, recv, shard, tensor=None):
        return pltpu.make_async_remote_copy(
            src_ref=src, dst_ref=dst, send_sem=send, recv_sem=recv,
            device_id=(shard, t if tensor is None else tensor), device_id_type=MESH,
        )

    def wait_bytes(ref, sem):
        pltpu.make_async_copy(ref, ref, sem).wait()

    loads = [
        pltpu.make_async_copy(grads_hbm, grads_ref, in_s.at[0]),
        pltpu.make_async_copy(w_hbm, w_ref, in_s.at[1]),
        pltpu.make_async_copy(acts_hbm, acts_ref, in_s.at[2]),
    ]
    for load in loads:
        load.start()

    barrier = pltpu.get_barrier_semaphore()

    @pl.loop(0, 32)
    def _(i):
        @pl.when(i != s)
        def _():
            pl.semaphore_signal(barrier, inc=1, device_id=(i, t), device_id_type=MESH)

    for d in range(1, 4):
        pl.semaphore_signal(barrier, inc=1, device_id=(s, (t + d) % 4), device_id_type=MESH)
        pl.semaphore_signal(barrier, inc=1, device_id=(pair, (t + d) % 4), device_id_type=MESH)

    is_gowner = h == t % 2
    sibling = t + 1 - 2 * (t % 2)
    along = 2 * h + t // 2

    def chip(step):
        there = (along + step) % 4
        return z * 8 + x * 2 + there // 2, 2 * (there % 2) + there // 2

    @pl.when(is_gowner)
    def _():
        pl.semaphore_signal(barrier, inc=1, device_id=chip(1), device_id_type=MESH)
        pl.semaphore_signal(barrier, inc=1, device_id=chip(3), device_id_type=MESH)


    hots = []
    for m in range(2):
        token = lax.broadcasted_iota(jnp.int32, (256, 128), 0)
        hots.append(jnp.where(token == idx_ref[m:m + 1, :], 1.0, 0.0).astype(BF16))
    loads[0].wait()
    for m in range(2):
        rows = slice(128 * m, 128 * m + 128)
        pg = dot_tn(hots[m], grads_ref[m]).astype(BF16)
        gpicked[rows, 0:DOUT] = pg
        gpicked[rows, DOUT:DOUT + 512] = pg[:, 0:512]
    for i in range(2):
        at = pl.multiple_of(128 * (2 * t + i), 128)
        strip = dot_tn(gpicked[:, pl.ds(at, 128)], gpicked[:, pl.ds(at, GBAND)])
        gq[128 * i:128 * i + 128, :] = (strip * scale).astype(BF16)

    loads[1].wait()
    for j in range(NT - 1):
        w2[0, j] = w_ref[:, 128 * j:128 * j + 128]
        w2[1, j] = w_ref[:, WIDTH + 128 * j:WIDTH + 128 * j + 128]
    cut = w_ref[:, SPLIT:WIDTH].astype(F32)
    w2[0, NT - 1] = jnp.where(lane < EDGE, cut, 0.0).astype(BF16)
    edge[0:32, 0:128] = jnp.where(lane >= EDGE, cut, 0.0)
    edge[0:32, 0:TAIL] = w_ref[:, 2688:2736].astype(F32)
    w2[1, NT - 1] = edge[0:32, 0:128].astype(BF16)
    wpair[:, pl.ds(pl.multiple_of(32 * h, 32), 32), :] = w2[h]

    @pl.when(is_gowner)
    def _():
        pl.semaphore_wait(barrier, 39)

    @pl.when(jnp.logical_not(is_gowner))
    def _():
        pl.semaphore_wait(barrier, 37)


    g_lane = t % 2

    @pl.loop(0, 16)
    def _(i):
        to = 2 * i + g_lane

        @pl.when(to != s)
        def _():
            copy_to(gq.at[pl.ds(pl.multiple_of(GROWS * i, GROWS), GROWS)], grecv.at[s],
                    grs_s.at[i], grs_r.at[0], to).start()

    for b in range(2):
        @pl.loop(0, NT)
        def _(j):
            to = 2 * j + b

            @pl.when(to != s)
            def _():
                copy_to(w2.at[b, j], wc.at[pl.ds(pl.multiple_of(32 * s, 32), 32)],
                        wa_s.at[b * NT + j], wa_r.at[0], to).start()

    active = o < NT

    @pl.when(active)
    def _():
        wc[pl.ds(pl.multiple_of(32 * s, 32), 32), :] = w2[h, jnp.minimum(o, NT - 1)]

    wp_copy = copy_to(w2.at[1 - h], wpair.at[:, pl.ds(pl.multiple_of(32 * h, 32), 32), :],
                      one_s.at[0], one_r.at[0], pair)
    wp_copy.start()

    @pl.when(is_gowner)
    def _():
        grecv[s] = gq[pl.ds(pl.multiple_of(GROWS * o, GROWS), GROWS), :]

    def ring_ids(axis):
        if axis == 0:
            return x, z * 8 + ((x + 1) % 4) * 2 + h, z * 8 + ((x + 3) % 4) * 2 + h
        return z, ((z + 1) % 4) * 8 + x * 2 + h, ((z + 3) % 4) * 8 + x * 2 + h

    part[0, 2, 3, 64:96] = jnp.zeros((32, BAND), BF16)
    part[0, 3, 3] = jnp.zeros((96, BAND), BF16)
    part[1, 3, 2, 64:96] = jnp.zeros((32, BAND), BF16)
    part[1, 3, 3] = jnp.zeros((96, BAND), BF16)

    pending = []
    loads[2].wait()
    high = lax.broadcasted_iota(jnp.int32, (128, 1), 0) >= EDGE

    def ring(k, src, dst, to):
        c = copy_to(src, dst, ring_s.at[k], ring_r.at[k], to)
        c.start()
        pending.append(c)
        return c

    phase1 = []
    for c in range(2):
        for m in range(2):
            cols_m = slice(128 * m, 128 * m + 128)
            if c == 0:
                pa = dot(acts_ref[m, 0:WIDTH, :], hots[m])
                picked[c, 0:SPLIT, cols_m] = pa[0:SPLIT].astype(BF16)
                cut = pa[SPLIT:WIDTH]
                picked[c, SPLIT:WIDTH, cols_m] = jnp.where(high, 0.0, cut).astype(BF16)
                edge[:, cols_m] = jnp.where(high, cut, 0.0)
            else:
                pa = dot(acts_ref[m, WIDTH:2 * ABLK, :], hots[m])
                picked[c, 0:SPLIT, cols_m] = pa[0:SPLIT].astype(BF16)
                edge[0:TAIL, cols_m] = pa[SPLIT:SPLIT + TAIL]
                picked[c, SPLIT:WIDTH, cols_m] = edge[:, cols_m].astype(BF16)
        picked[c, WIDTH:WIDTH + 640, :] = picked[c, 0:640, :]

        @pl.loop(0, NT)
        def _(i):
            at = pl.multiple_of(128 * i, 128)
            strip = dot_nt(picked[c, pl.ds(at, 128), :], picked[c, pl.ds(at, BAND), :])
            strip = (strip * scale).astype(BF16)
            for q in range(4):
                u = 4 * i + q
                oo = u // 3
                row = pl.multiple_of((u % 3) * 32, 32)
                zz, xx = oo // 4, oo % 4
                piece = strip[32 * q:32 * q + 32]
                if c == 0:
                    part[0, xx, zz, pl.ds(row, 32), :] = piece
                else:
                    part[1, zz, xx, pl.ds(row, 32), :] = piece

        if c == 0:
            @pl.when(is_gowner)
            def _():
                wait_bytes(grecv.at[pl.ds(0, 31)], grs_r.at[0])
                acc = grecv[0].astype(F32)
                for i in range(1, 32):
                    acc = acc + grecv[i].astype(F32)
                gall[pl.ds(pl.multiple_of(256 * t + GROWS * o, GROWS), GROWS), :] = acc.astype(BF16)

                @pl.loop(0, 16)
                def _(i):
                    @pl.when(i != o)
                    def _():
                        mine = gall.at[pl.ds(pl.multiple_of(256 * t + GROWS * o, GROWS), GROWS)]
                        copy_to(mine, mine, gag_s.at[i], gag_r.at[0], 2 * i + h).start()

        pos, right, left_id = ring_ids(c)
        far, nxt, prv = (pos + 2) % 4, (pos + 1) % 4, (pos + 3) % 4
        k = 6 * c
        top, bottom = pl.ds(0, HALF), pl.ds(HALF, HALF)
        phase1.append([
            ring(k + 0, part.at[c, far, :, top], rb1.at[c, 0], right),
            ring(k + 1, part.at[c, far, :, bottom], rb1.at[c, 1], left_id),
            ring(k + 2, part.at[c, nxt, :, bottom], rb1.at[c, 2], right),
            ring(k + 3, part.at[c, prv, :, top], rb1.at[c, 3], left_id),
        ])

    def add2(a, b):
        return a.astype(F32) + b.astype(F32)

    def add3(a, b, c):
        return a.astype(F32) + b.astype(F32) + c.astype(F32)

    def quarter(step):
        return gall.at[pl.ds(pl.multiple_of(256 * chip(step)[1], 256), 256)]

    def half_quarter(step, side):
        return gall.at[pl.ds(pl.multiple_of(256 * chip(step)[1] + 128 * side, 128), 128)]

    def along_y(k, ref, to):
        copy_to(ref, ref, gx_s.at[k], gx_r.at[k], *to).start()

    @pl.when(is_gowner)
    def _():
        wait_bytes(gall.at[pl.ds(0, 240)], gag_r.at[0])
        along_y(0, quarter(0), chip(1))
        along_y(1, quarter(0), chip(3))
        along_y(2, quarter(0), (s, sibling))

    order1 = (2, 1, 3, 0)
    combined = []
    for c in range(2):
        pos, right, left_id = ring_ids(c)
        nxt, prv = (pos + 1) % 4, (pos + 3) % 4
        k = 6 * c
        second = ring_ids(1 - c)[0]
        phase1[c][0].wait_recv()
        phase1[c][1].wait_recv()
        tail = []
        for n, step in enumerate(order1):
            q = (second + step) % 4
            st1[c, 0, q] = add2(rb1[c, 0, q], part[c, nxt, q, 0:HALF]).astype(BF16)
            st1[c, 1, q] = add2(rb1[c, 1, q], part[c, prv, q, HALF:ROWS]).astype(BF16)
            tail.append((
                ring(57 + 8 * c + n, st1.at[c, 0, q], rb1.at[c, 4, q], right),
                ring(61 + 8 * c + n, st1.at[c, 1, q], rb1.at[c, 5, q], left_id),
            ))
        combined.append(tail)

    phase2 = [[], []]
    for n, step in enumerate(order1):
        for c in range(2):
            pos = ring_ids(c)[0]
            second, right, left_id = ring_ids(1 - c)
            q = (second + step) % 4
            if n == 0:
                phase1[c][2].wait_recv()
                phase1[c][3].wait_recv()
            combined[c][n][0].wait_recv()
            combined[c][n][1].wait_recv()
            r1[c, q, 0:HALF] = add3(part[c, pos, q, 0:HALF], rb1[c, 4, q], rb1[c, 3, q]).astype(BF16)
            r1[c, q, HALF:ROWS] = add3(part[c, pos, q, HALF:ROWS], rb1[c, 5, q], rb1[c, 2, q]).astype(BF16)
            k = 12 + 6 * c
            if step == 2:
                phase2[c].append(ring(k + 0, r1.at[c, q, top], rb2.at[c, 0], right))
                phase2[c].append(ring(k + 1, r1.at[c, q, bottom], rb2.at[c, 1], left_id))
            elif step == 1:
                phase2[c].append(ring(k + 2, r1.at[c, q, bottom], rb2.at[c, 2], right))
            elif step == 3:
                phase2[c].append(ring(k + 3, r1.at[c, q, top], rb2.at[c, 3], left_id))
    for c in range(2):
        pos, right, left_id = ring_ids(1 - c)
        nxt, prv = (pos + 1) % 4, (pos + 3) % 4
        k = 12 + 6 * c
        phase2[c][0].wait_recv()
        st2[c, 0] = add2(rb2[c, 0], r1[c, nxt, 0:HALF]).astype(BF16)
        phase2[c].append(ring(k + 4, st2.at[c, 0], rb2.at[c, 4], right))
        phase2[c][1].wait_recv()
        st2[c, 1] = add2(rb2[c, 1], r1[c, prv, HALF:ROWS]).astype(BF16)
        phase2[c].append(ring(k + 5, st2.at[c, 1], rb2.at[c, 5], left_id))
    @pl.when(is_gowner)
    def _():
        wait_bytes(quarter(3), gx_r.at[0])
        along_y(3, half_quarter(3, 0), chip(1))
        along_y(5, quarter(3), (s, sibling))
        wait_bytes(quarter(1), gx_r.at[1])
        along_y(4, half_quarter(1, 1), chip(3))
        along_y(6, quarter(1), (s, sibling))
        wait_bytes(half_quarter(2, 0), gx_r.at[3])
        wait_bytes(half_quarter(2, 1), gx_r.at[4])
        along_y(7, quarter(2), (s, sibling))

    for c in range(2):
        pos, right, left_id = ring_ids(1 - c)
        for cp in phase2[c][2:]:
            cp.wait_recv()
        r2[c, 0:HALF] = add3(r1[c, pos, 0:HALF], rb2[c, 4], rb2[c, 3]).astype(BF16)
        r2[c, HALF:ROWS] = add3(r1[c, pos, HALF:ROWS], rb2[c, 5], rb2[c, 2]).astype(BF16)

    hx = ring(24, r2.at[1 - h], r3, pair)
    @pl.when(jnp.logical_not(is_gowner))
    def _():
        for k in (2, 5, 6, 7):
            wait_bytes(gall.at[pl.ds(0, 256)], gx_r.at[k])

    eye = lax.broadcasted_iota(jnp.int32, (128, 128), 0) == lax.broadcasted_iota(jnp.int32, (128, 128), 1)

    def unpack(src, dst, tiles, band, double):
        bands = band // 128
        column = lax.broadcasted_iota(jnp.int32, (1, band), 1) // 128
        weight = jnp.where(jnp.logical_and(column > 0, column <= double), 2.0, 1.0)

        def body(i, carry):
            square, trace = carry
            at = pl.multiple_of(128 * i, 128)
            strip = src[pl.ds(at, 128), :]
            wide = strip.astype(F32)
            square = square + fold_rows(wide * wide) * weight
            trace = trace + fold_rows(jnp.where(eye, wide[:, 0:128], 0.0))
            for k in range(bands):
                to = pl.multiple_of(128 * ((i + k) % tiles), 128)
                dst[pl.ds(at, 128), pl.ds(to, 128)] = strip[:, 128 * k:128 * k + 128]
                if 1 <= k <= double:
                    dst[pl.ds(to, 128), pl.ds(at, 128)] = wide[:, 128 * k:128 * k + 128].T.astype(BF16)
            return square, trace

        square, trace = lax.fori_loop(
            0, tiles, body, (jnp.zeros((8, band), F32), jnp.zeros((8, 128), F32)))
        return total(square), total(trace)

    def norms(square, trace, width):
        shift = DAMPING * trace / width
        return shift, 1.0 / jnp.sqrt(square + 2.0 * shift * trace + shift * shift * width)

    @pl.when(active)
    def _():
        square, trace = unpack(gall, gfull, GT, GBAND, 3)
        shift, inv = norms(square, trace, float(DOUT))
        wait_bytes(wc.at[pl.ds(0, 31 * 32)], wa_r.at[0])
        y0 = wc[...].astype(F32)
        y1 = (dot(gfull[...], wc[...]) + shift * y0) * inv
        left[...] = y1.astype(BF16)
        y2 = (dot(gfull[...], left[...]) + shift * y1) * inv
        left[...] = y2.astype(BF16)
        y3 = (dot(gfull[...], left[...]) + shift * y2) * inv
        left[...] = (4.0 * y0 - 6.0 * y1 + 4.0 * y2 - y3).astype(BF16)
        vt[o] = left[pl.ds(pl.multiple_of(64 * o, 64), 64), :]

        @pl.loop(0, 16)
        def _(i):
            @pl.when(i != o)
            def _():
                copy_to(left.at[pl.ds(pl.multiple_of(64 * i, 64), 64)], vt.at[o],
                        lf_s.at[i], lf_r.at[0], 2 * i + h).start()

    hx.wait_recv()
    ag[pl.ds(pl.multiple_of(ROWS * o, ROWS), ROWS), :] = add2(r2[h], r3[...]).astype(BF16)

    def piece(axis, first, second, k):
        zz, xx = (second, first) if axis == 0 else (first, second)
        return ag.at[pl.ds(pl.multiple_of(ROWS * (4 * zz + xx) + HALF * k, HALF), HALF)]

    def cols(ref, side):
        return ref.at[:, pl.ds(384 * side, 384)]

    lines = []
    for k in range(2):
        pa, ra, la = ring_ids(k)
        pb, rb, lb = ring_ids(1 - k)
        base = 25 + 16 * k
        own = piece(k, pa, pb, k)
        lines.append({"a": [ring(base, own, own, ra), ring(base + 1, own, own, la)], "r": [], "l": []})

    def send_b(k, n, first):
        pb, rb, lb = ring_ids(1 - k)
        base = 25 + 16 * k
        p = piece(k, first, pb, k)
        lines[k]["r"].append(ring(base + 4 + n, p, p, rb))
        lines[k]["l"].append(ring(base + 8 + n, p, p, lb))

    for k in range(2):
        send_b(k, 0, ring_ids(k)[0])
    for k in range(2):
        pa, ra, la = ring_ids(k)
        pb = ring_ids(1 - k)[0]
        base = 25 + 16 * k
        lines[k]["a"][0].wait_recv()
        p = cols(piece(k, (pa + 3) % 4, pb, k), 0)
        lines[k]["a"].append(ring(base + 2, p, p, ra))
        lines[k]["a"][1].wait_recv()
        p = cols(piece(k, (pa + 1) % 4, pb, k), 1)
        lines[k]["a"].append(ring(base + 3, p, p, la))
    for k in range(2):
        pa = ring_ids(k)[0]
        send_b(k, 1, (pa + 3) % 4)
        send_b(k, 2, (pa + 1) % 4)
    for k in range(2):
        pa = ring_ids(k)[0]
        lines[k]["a"][2].wait_recv()
        lines[k]["a"][3].wait_recv()
        send_b(k, 3, (pa + 2) % 4)
    order = (0, 3, 1, 2)
    for n in range(2):
        for k in range(2):
            pa = ring_ids(k)[0]
            pb, rb, lb = ring_ids(1 - k)
            base = 25 + 16 * k
            lines[k]["r"][n].wait_recv()
            p = piece(k, (pa + order[n]) % 4, (pb + 3) % 4, k)
            lines[k]["a"].append(ring(base + 12 + n, p, p, rb))

    for n in range(2, 4):
        for k in range(2):
            pa = ring_ids(k)[0]
            pb, rb, lb = ring_ids(1 - k)
            base = 25 + 16 * k
            lines[k]["l"][n].wait_recv()
            p = piece(k, (pa + order[n]) % 4, (pb + 1) % 4, k)
            lines[k]["a"].append(ring(base + 12 + n, p, p, lb))
    for k in range(2):
        for n in range(2, 4):
            lines[k]["r"][n].wait_recv()
        for n in range(2):
            lines[k]["l"][n].wait_recv()
        for cp in lines[k]["a"][4:]:
            cp.wait_recv()

    square, trace = unpack(ag, sfull, NT, BAND, 5)
    shift, inv = norms(square, trace, float(ABLK))

    @pl.when(active)
    def _():
        wait_bytes(vt.at[pl.ds(0, NT - 1)], lf_r.at[0])

    @pl.when(jnp.logical_not(active))
    def _():
        wait_bytes(vt, lf_r.at[0])

    for j in range(NT):
        vfull[:, 128 * j:128 * j + 128] = vt[j]
    y0 = vfull[...].astype(F32)
    y1 = (dot(vfull[...], sfull[...]) + shift * y0) * inv
    vfull[...] = y1.astype(BF16)
    upd[...] = 4.0 * y0 - 6.0 * y1
    y2 = (dot(vfull[...], sfull[...]) + shift * y1) * inv
    vfull[...] = y2.astype(BF16)
    upd[...] = upd[...] + 4.0 * y2
    y3 = (dot(vfull[...], sfull[...]) + shift * y2) * inv
    upd[...] = upd[...] - y3

    wp_copy.wait_recv()
    acc = jnp.zeros((64, 128), F32)
    for j in range(NT):
        acc = acc + upd[:, 128 * j:128 * j + 128] * wpair[j].astype(F32)
    al[0] = fold_rows(acc)
    here = 4 * h + t
    al1[here] = al[0]
    sums = []
    for d in range(1, 8):
        there = (here + d) % 8
        g = copy_to(al.at[0], al1.at[here], a1_s.at[d], a1_r.at[d], 2 * o + there // 4, there % 4)
        g.start()
        sums.append(g)
    for g in sums:
        g.wait_recv()
    acc = al1[0]
    for i in range(1, 8):
        acc = acc + al1[i]
    al[1] = acc
    al2[o] = acc

    @pl.loop(0, 16)
    def _(i):
        @pl.when(i != o)
        def _():
            copy_to(al.at[1], al2.at[o], a2_s.at[i], a2_r.at[0], 2 * i + h).start()

    ub[...] = upd[pl.ds(pl.multiple_of(32 * (1 - h), 32), 32), :].astype(BF16)
    u_copy = copy_to(ub, ux, one_s.at[1], one_r.at[1], pair)
    u_copy.start()
    u_copy.wait_recv()
    own = upd[pl.ds(pl.multiple_of(32 * h, 32), 32), :]
    other = ux[...].astype(F32)
    b0 = jnp.where(h == 0, own, other)
    b1 = jnp.where(h == 0, other, own)
    upd_out[:, 0:SPLIT] = b0[:, 0:SPLIT]
    upd_out[:, SPLIT:WIDTH] = jnp.where(lane < EDGE, b0[:, SPLIT:WIDTH], b1[:, SPLIT:WIDTH])
    upd_out[:, WIDTH:2688] = b1[:, 0:SPLIT]
    upd_out[:, 2688:2736] = b1[:, SPLIT:SPLIT + TAIL]

    wait_bytes(al2.at[pl.ds(0, 15)], a2_r.at[0])
    acc = al2[0]
    for i in range(1, 16):
        acc = acc + al2[i]
    ratio = jnp.minimum(1.0, CLIP_LEVEL / jnp.sqrt(total(acc) / (DOUT * FF)))
    upd_out[...] = upd_out[...] * ratio

    for cp in pending + sums + [wp_copy, u_copy]:
        cp.wait_send()

    @pl.when(is_gowner)
    def _():
        for k in range(8):
            wait_bytes(gall.at[pl.ds(0, 128 if k in (3, 4) else 256)], gx_s.at[k])

    @pl.loop(0, 16)
    def _(i):
        @pl.when(2 * i + g_lane != s)
        def _():
            wait_bytes(gq.at[pl.ds(0, GROWS)], grs_s.at[i])

        @pl.when(jnp.logical_and(active, i != o))
        def _():
            wait_bytes(left.at[pl.ds(0, 64)], lf_s.at[i])

        @pl.when(i != o)
        def _():
            wait_bytes(al.at[1], a2_s.at[i])

        @pl.when(jnp.logical_and(is_gowner, i != o))
        def _():
            wait_bytes(gall.at[pl.ds(0, GROWS)], gag_s.at[i])

    for b in range(2):
        @pl.loop(0, NT)
        def _(j):
            @pl.when(2 * j + b != s)
            def _():
                wait_bytes(w2.at[b, j], wa_s.at[b * NT + j])


def whole_step(sample_idx, out_grads, grad_weight, hidden_acts):
    dma = pltpu.SemaphoreType.DMA
    vmem = pltpu.VMEM
    return pl.pallas_call(
        kernel,
        out_shape=jax.ShapeDtypeStruct((MINE, 2 * ABLK), F32),
        in_specs=[pl.BlockSpec(memory_space=pltpu.VMEM)] + [pl.BlockSpec(memory_space=pl.ANY)] * 3,
        out_specs=pl.BlockSpec(memory_space=pltpu.VMEM),
        scratch_shapes=[
            vmem((2, 256, DOUT), BF16),
            vmem((MINE, 2 * ABLK), BF16),
            vmem((2, 2 * ABLK, 256), BF16),
            vmem((2, WIDTH + 640, 256), BF16),
            vmem((256, DOUT + 512), BF16),
            vmem((2, 4, 4, ROWS, BAND), BF16),
            vmem((2, NT, 32, 128), BF16),
            vmem((NT, 64, 128), BF16),
            vmem((DOUT, 128), BF16),
            vmem((128, 256), F32),
            vmem((256, GBAND), BF16),
            vmem((32, GROWS, GBAND), BF16),
            vmem((DOUT, GBAND), BF16),
            vmem((DOUT, DOUT), BF16),
            vmem((2, 6, 4, HALF, BAND), BF16),
            vmem((2, 2, 4, HALF, BAND), BF16),
            vmem((2, 4, ROWS, BAND), BF16),
            vmem((2, 6, HALF, BAND), BF16),
            vmem((2, 2, HALF, BAND), BF16),
            vmem((2, ROWS, BAND), BF16),
            vmem((ROWS, BAND), BF16),
            vmem((16 * ROWS, BAND), BF16),
            vmem((WIDTH, WIDTH), BF16),
            vmem((NT, 64, 128), BF16),
            vmem((64, WIDTH), BF16),
            vmem((DOUT, 128), BF16),
            vmem((64, WIDTH), F32),
            vmem((32, WIDTH), BF16),
            vmem((32, WIDTH), BF16),
            vmem((2, 8, 128), F32),
            vmem((8, 8, 128), F32),
            vmem((16, 8, 128), F32),
            dma((16,)), dma((1,)),
            dma((16,)), dma((1,)),
            dma((8,)), dma((8,)),
            dma((2 * NT,)), dma((1,)),
            dma((16,)), dma((1,)),
            dma((73,)), dma((73,)),
            dma((8,)), dma((8,)),
            dma((16,)), dma((1,)),
            dma((2,)), dma((2,)), dma((3,)),
        ],
        compiler_params=pltpu.CompilerParams(
            collective_id=0, has_side_effects=True, vmem_limit_bytes=60 * 1024 * 1024),
    )(sample_idx, out_grads, grad_weight, hidden_acts)


def per_device(hidden_acts, out_grads, sample_idx, grad_weight, momentum, weight):
    scaled = whole_step(sample_idx, out_grads, grad_weight, jnp.swapaxes(hidden_acts, 1, 2))
    new_momentum = MOMENTUM_RATE * momentum + scaled
    new_weight = weight - LEARN_RATE * new_momentum
    return (new_momentum, new_weight)


def solution(mesh):
    in_specs = (
        P(None, "shard", "tensor"),
        P(None, "shard", None),
        P(None, "shard"),
        P("shard", "tensor"),
        P("shard", "tensor"),
        P("shard", "tensor"),
    )
    out_specs = (P("shard", "tensor"), P("shard", "tensor"))
    return jax.shard_map(
        per_device, mesh=mesh, in_specs=in_specs, out_specs=out_specs, check_vma=False
    )
```
